256 devices in a mesh: dp: 8 (over y, core), expert: 32 (over z, x).
Axes of the slice: x: 4, y: 4, z: 8, core: 2. Of those that a mesh axis runs over, the one named last changes fastest.
Arguments:
- qkv: bfloat16 [256, 128, 6144], P(('dp', 'expert')), may hold values from -6 to 6
- resid: bfloat16 [256, 128, 2048], P(('dp', 'expert')), may hold values from -54 to 54
- lengths: int32 [256], P(('dp', 'expert')), may hold values from 32 to 128
- norm_gain: float32 [2048], replicated, may hold values from 0.25 to 1.75
- expert_ids: int32 [256, 128, 2], P(('dp', 'expert')), may hold values from 0 to 31, all different within a row; in each aligned block of 128 rows (0 to 127, 128 to 255, ..., all dimensions but the last counted through in order) at most 16 rows name the same one
- gate_vals: bfloat16 [256, 128, 2], P(('dp', 'expert')), may hold values from 0.099609375 to 1
- w_gate: bfloat16 [32, 768, 2048], P('expert', None, 'dp'), may hold values from -0.125 to 0.125
- w_up: bfloat16 [32, 768, 2048], P('expert', None, 'dp'), may hold values from -0.125 to 0.125
- w_down: bfloat16 [32, 768, 2048], P('expert', None, 'dp'), may hold values from -0.21875 to 0.21875
- cotangent: bfloat16 [256, 128, 2048], P(('dp', 'expert')), may hold values from -6 to 6
Outputs:
- mixture: bfloat16 [256, 128, 2048], P(('dp', 'expert'))
- grad_stream: float32 [256, 128, 2048], P(('dp', 'expert'))
- grad_gate: float32 [32, 768, 2048], P('expert', None, 'dp')
- grad_up: float32 [32, 768, 2048], P('expert', None, 'dp')
- grad_down: float32 [32, 768, 2048], P('expert', None, 'dp')
The draws below stay inside these ranges and needn't reach their ends.
Inputs may be any that keep to these rules, and one draw needn't show every extreme that they name: `expert_ids`: among the 128 tokens of one device, no expert is named by more than 16 routes, a bound that some block reaches; the 2 ids of a token differ.
All inputs are finite; a program needn't handle non-finite values.
Results may differ from the reference program's by a relative error of at most 0.015.
Values may be sent and summed in bfloat16 or wider, within the bound.
No kernel may reach another device: no remote copies, remote signals or barrier semaphores. Data moves between devices by JAX's collectives and lax.ppermute only.
A program may use at most 128 MiB of HBM per device.

```python
import math
import jax
import jax.numpy as jnp
import numpy as np
from jax import lax

D = 2048
HEADS = 16
HEAD = 128
FF = 768
TOP = 2
STEPS = 128
EXPERTS = 32
SERIES = 256
TOK_DEV = 128
GROUP = 32
CAP = 16
N_DP = 8
N_EXPERT = 32


def draw_qkv(key, part):
    first = jax.random.fold_in(key, 0)
    shape = (SERIES, STEPS, 3 * D)
    values = jnp.clip(jax.random.normal(first, shape, jnp.float32), -6.0, 6.0)
    return values.astype(jnp.bfloat16)


def draw_resid(key, part):
    first, second, third = jax.random.split(key, 3)
    shape = (SERIES, STEPS, D)
    columns = jnp.exp(jax.random.uniform(second, (D,), jnp.float32, math.log(0.3), math.log(3.0)))
    tokens = jnp.exp(jax.random.uniform(third, (SERIES, STEPS, 1), jnp.float32, math.log(0.3), math.log(3.0)))
    base = jnp.clip(jax.random.normal(first, shape, jnp.float32), -6.0, 6.0)
    return (base * columns * tokens).astype(jnp.bfloat16)


def draw_lengths(key, part):
    first, second = jax.random.split(key, 2)
    values = jax.random.randint(first, (SERIES,), STEPS // 4, STEPS + 1, jnp.int32)
    order = jax.random.permutation(second, SERIES)
    values = values.at[order[0]].set(STEPS).at[order[1]].set(STEPS // 4)
    return values.astype(jnp.int32)


def shard_levels(own_key, dims, pieces, low, top_value):
    level = 1.0
    for dim, blocks in pieces:
        heights = jax.random.uniform(jax.random.fold_in(jax.random.fold_in(own_key, 6), dim), (blocks,), jnp.float32, low / len(pieces), top_value / len(pieces))
        level = level * jnp.repeat(jnp.exp(heights), dims[dim] // blocks).reshape((-1,) + (1,) * (len(dims) - 1 - dim))
    return level


def routed_block(own_key, own, number, rows, amount, top, reach, slope):
    sequence = jax.random.permutation(own_key, amount)
    crowded, common = portions_of(amount, rows * top, reach, slope, True), portions_of(amount, rows * top, reach, slope, False)
    places = jnp.arange(amount)

    def named(sizes, rotation):
        used = int((sizes > 0).sum())
        fixed = max(1, used // 4)
        passed = fixed + (places - fixed + rotation * (used - fixed)) % max(1, amount - fixed)
        return jnp.zeros((amount,), jnp.int32).at[sequence[jnp.where(places < fixed, places, passed)]].set(jnp.asarray(sizes, jnp.int32))

    sizes = jnp.where(number % 4 == 0, named(crowded, number // 4), named(common, number - number // 4 - 1))
    mixed = jax.random.permutation(jax.random.fold_in(own, 3), amount)
    giver, sink = mixed[0:amount // 2 * 2:2], mixed[1:amount // 2 * 2:2]
    room = jnp.minimum(sizes[giver] - 1, reach - sizes[sink]) // 2
    room = jnp.where((giver == sequence[0]) | (sink == sequence[0]) | (sizes[sink] == 0), 0, jnp.maximum(room, 0))
    passed = jax.random.randint(jax.random.fold_in(own, 4), (amount // 2,), 0, 1 << 20) % (room + 1)
    sizes = sizes.at[giver].add(-passed).at[sink].add(passed)
    members = jnp.searchsorted(jnp.cumsum(sizes), jnp.arange(rows * top), side="right").astype(jnp.int32)
    listing = members.reshape(top, rows).T
    listing = listing[jax.random.permutation(jax.random.fold_in(own, 1), rows)]
    rotation = jax.random.randint(jax.random.fold_in(own, 2), (rows, 1), 0, top)
    return jnp.take_along_axis(listing, (jnp.arange(top)[None, :] + rotation) % top, axis=1)


def portions_of(amount, total, reach, lean, full):
    weights = [(1 << 20) // math.isqrt(standing ** lean) + 1 for standing in range(1, amount + 1)]
    largest = reach if full else min(reach, max(-(-total // amount), total * weights[0] // sum(weights)))
    least = 1 if total - largest >= amount - 1 else 0
    holding, rest = [largest] + [least] * (amount - 1), total - largest - least * (amount - 1)
    while rest > 0:
        candidates = [i for i in range(1, amount) if holding[i] < largest] or [i for i in range(1, amount) if holding[i] < reach]
        whole, remaining = sum([weights[i] for i in candidates]), rest
        for i in candidates:
            addition = min(reach - holding[i], max(1, remaining * weights[i] // whole), rest)
            holding[i] = holding[i] + addition
            rest = rest - addition
    return np.array(holding)


def scatter_about(own_key, extent, scale, limit, pieces=(), held_as=jnp.bfloat16):
    loudness = shard_levels(own_key, extent, pieces, -0.22, 0.18) if pieces else 1.0
    entries = jax.random.normal(own_key, extent, jnp.float32) * scale * loudness
    return jnp.minimum(jnp.maximum(entries, -limit), limit).astype(held_as)


def setup_inputs(seed: int = 0) -> dict:
    arg_keys = jax.random.split(jax.random.key(seed), 11)
    qkv = draw_qkv(jax.random.fold_in(arg_keys[10], 71), 0)
    resid = draw_resid(jax.random.fold_in(arg_keys[10], 71), 0)
    lengths = draw_lengths(jax.random.fold_in(arg_keys[10], 71), 0)
    norm_gain = jnp.clip(1.0 + 0.15 * jax.random.normal(arg_keys[3], (D,), jnp.float32), 0.25, 1.75)
    expert_ids_keys = jax.random.split(jax.random.fold_in(arg_keys[4], 1), SERIES * STEPS // TOK_DEV)
    expert_ids_turns = jax.random.permutation(jax.random.fold_in(arg_keys[4], 3), SERIES * STEPS // TOK_DEV)
    expert_ids = jax.vmap(lambda own, number: routed_block(jax.random.fold_in(arg_keys[4], 2), own, number, TOK_DEV, EXPERTS, TOP, CAP, 1))(expert_ids_keys, expert_ids_turns).reshape((SERIES, STEPS, TOP))
    gate_vals = jnp.clip(0.099609375 + 0.9003906 * jax.random.uniform(arg_keys[5], (SERIES, STEPS, TOP), jnp.float32) ** shard_levels(arg_keys[5], (SERIES, STEPS, TOP), ((0, 256),), -0.2, 0.2), 0.099609375, 1.0).astype(jnp.bfloat16)
    w_gate = scatter_about(arg_keys[6], (EXPERTS, FF, D), D ** -0.5, 0.125, ((0, 32), (2, 8)))
    w_up = scatter_about(arg_keys[7], (EXPERTS, FF, D), D ** -0.5, 0.125, ((0, 32), (2, 8)))
    w_down = scatter_about(arg_keys[8], (EXPERTS, FF, D), FF ** -0.5, 0.21875, ((0, 32), (2, 8)))
    cotangent = scatter_about(arg_keys[9], (SERIES, STEPS, D), 1.0, 6.0, ((0, 256),))
    return {"qkv": qkv, "resid": resid, "lengths": lengths, "norm_gain": norm_gain, "expert_ids": expert_ids, "gate_vals": gate_vals, "w_gate": w_gate, "w_up": w_up, "w_down": w_down, "cotangent": cotangent}


def attend(queries, key_rows, value_rows, live_mask):
    scores = jnp.einsum('sthc,uthc->thsu', queries.astype(jnp.float32), key_rows.astype(jnp.float32)) / math.sqrt(HEAD)
    count = queries.shape[0]
    self_pair = jnp.arange(count)[:, None] == jnp.arange(count)[None, :]
    allowed = jnp.transpose(live_mask)[:, None, None, :] | self_pair[None, None, :, :]
    masked = jnp.where(allowed, scores, -jnp.inf)
    highest = lax.optimization_barrier(jnp.max(masked, axis=-1, keepdims=True))
    raised = jnp.exp(masked - highest)
    weights = (raised / lax.optimization_barrier(jnp.sum(raised, axis=-1, keepdims=True))).astype(jnp.bfloat16)
    attended = jnp.einsum('thsu,uthc->sthc', weights.astype(jnp.float32), value_rows.astype(jnp.float32))
    attended = jnp.where(live_mask[:, :, None, None], attended, 0.0)
    return attended.astype(jnp.bfloat16)

def group_attend(inputs):
    packed, live_mask = inputs
    return attend(packed[:, :, 0], packed[:, :, 1], packed[:, :, 2], live_mask)

def expert_pass(inputs):
    x_rows, adjoint_rows, gate_rows, gate_weight, up_weight, down_weight = inputs
    gate_pre = jnp.dot(x_rows, gate_weight.T, preferred_element_type=jnp.float32)
    up_pre = jnp.dot(x_rows, up_weight.T, preferred_element_type=jnp.float32)
    sigmoid_gate = jax.nn.sigmoid(gate_pre)
    hidden = (gate_pre * sigmoid_gate * up_pre).astype(jnp.bfloat16)
    expert_out = jnp.dot(hidden, down_weight, preferred_element_type=jnp.float32).astype(jnp.bfloat16)
    grad_out = (gate_rows.astype(jnp.float32)[:, None] * adjoint_rows.astype(jnp.float32)).astype(jnp.bfloat16)
    grad_hidden = jnp.dot(grad_out, down_weight.T, preferred_element_type=jnp.float32)
    grad_gate_pre = (grad_hidden * up_pre * sigmoid_gate * (1.0 + gate_pre * (1.0 - sigmoid_gate))).astype(jnp.bfloat16)
    grad_up_pre = (grad_hidden * gate_pre * sigmoid_gate).astype(jnp.bfloat16)
    part_gate = jnp.dot(grad_gate_pre.T, x_rows, preferred_element_type=jnp.float32).astype(jnp.bfloat16)
    part_up = jnp.dot(grad_up_pre.T, x_rows, preferred_element_type=jnp.float32).astype(jnp.bfloat16)
    part_down = jnp.dot(hidden.T, grad_out, preferred_element_type=jnp.float32).astype(jnp.bfloat16)
    grad_rows = jnp.dot(grad_gate_pre, gate_weight, preferred_element_type=jnp.float32)
    grad_rows = (grad_rows + jnp.dot(grad_up_pre, up_weight, preferred_element_type=jnp.float32)).astype(jnp.bfloat16)
    return (expert_out, grad_rows, part_gate, part_up, part_down)

def reference(qkv, resid, lengths, norm_gain, expert_ids, gate_vals, w_gate, w_up, w_down, cotangent):
    packed = qkv.reshape(N_DP, GROUP, STEPS, 3, HEADS, HEAD)
    present = (jnp.arange(STEPS, dtype=jnp.int32)[None, :] < lengths[:, None]).reshape(N_DP, GROUP, STEPS)
    attended = lax.map(group_attend, (packed, present))
    stream = resid.astype(jnp.float32) + attended.reshape(SERIES, STEPS, D).astype(jnp.float32)
    inverse = 1.0 / jnp.sqrt(lax.optimization_barrier(jnp.mean(stream * stream, axis=-1, keepdims=True)) + 1e-05)
    normed = (stream * inverse * norm_gain).astype(jnp.bfloat16)
    block_count = N_DP * N_EXPERT
    per_block = TOK_DEV * TOP
    slot_count = N_EXPERT * CAP
    route_ids = expert_ids.reshape(block_count, per_block).astype(jnp.int32)
    onehot = (route_ids[:, :, None] == jnp.arange(EXPERTS, dtype=jnp.int32)[None, None, :]).astype(jnp.int32)
    running = jnp.cumsum(onehot, axis=1, dtype=jnp.int32) - 1
    position = lax.optimization_barrier(jnp.sum(running * onehot, axis=2, dtype=jnp.int32)).astype(jnp.int32)
    source = (jnp.arange(block_count, dtype=jnp.int32) % N_EXPERT)[:, None]
    slot_index = (route_ids * slot_count + source * CAP + position).astype(jnp.int32)
    group_tokens = GROUP * STEPS
    group_routes = group_tokens * TOP

    def group_pass(carry, inputs):
        normed_rows, adjoint_rows, gate_flat, index_flat = inputs
        filled = jnp.zeros((EXPERTS * slot_count,), jnp.int32).at[index_flat].set(jnp.arange(1, group_routes + 1, dtype=jnp.int32))
        token_of = jnp.where(filled > 0, (filled - 1) // TOP + 1, 0).astype(jnp.int32)
        normed_ext = jnp.concatenate([jnp.zeros((1, D), jnp.bfloat16), normed_rows], axis=0)
        adjoint_ext = jnp.concatenate([jnp.zeros((1, D), jnp.bfloat16), adjoint_rows], axis=0)
        gate_ext = jnp.concatenate([jnp.zeros((1,), jnp.bfloat16), gate_flat], axis=0)
        normed_buf = normed_ext[token_of].reshape(EXPERTS, slot_count, D)
        adjoint_buf = adjoint_ext[token_of].reshape(EXPERTS, slot_count, D)
        gate_buf = gate_ext[filled].reshape(EXPERTS, slot_count)
        out_buf, grad_buf, part_gate, part_up, part_down = lax.map(expert_pass, (normed_buf, adjoint_buf, gate_buf, w_gate, w_up, w_down))
        carry = (carry[0] + part_gate.astype(jnp.float32), carry[1] + part_up.astype(jnp.float32), carry[2] + part_down.astype(jnp.float32))
        out_route = out_buf.reshape(EXPERTS * slot_count, D)[index_flat].reshape(group_tokens, TOP, D)
        grad_route = grad_buf.reshape(EXPERTS * slot_count, D)[index_flat].reshape(group_tokens, TOP, D)
        gates = gate_flat.reshape(group_tokens, TOP).astype(jnp.float32)
        mixture = lax.optimization_barrier(jnp.sum(gates[:, :, None] * out_route.astype(jnp.float32), axis=1)).astype(jnp.bfloat16)
        grad_normed = lax.optimization_barrier(jnp.sum(grad_route.astype(jnp.float32), axis=1))
        return (carry, (mixture, grad_normed))
    empty = jnp.zeros((EXPERTS, FF, D), jnp.float32)
    inputs = (normed.reshape(N_DP, group_tokens, D), cotangent.reshape(N_DP, group_tokens, D), gate_vals.reshape(N_DP, group_routes), slot_index.reshape(N_DP, group_routes))
    grads, (mixture, grad_normed) = lax.scan(group_pass, (empty, empty, empty), inputs)
    mixture = mixture.reshape(SERIES, STEPS, D)
    grad_normed = grad_normed.reshape(SERIES, STEPS, D)
    scaled = norm_gain * grad_normed
    grad_stream = inverse * scaled - stream * inverse * inverse * inverse * lax.optimization_barrier(jnp.mean(stream * scaled, axis=-1, keepdims=True))
    return (mixture, grad_stream, grads[0], grads[1], grads[2])
```

```python
import functools
import math

import jax
import jax.numpy as jnp
from jax import lax
from jax.experimental import pallas as pl
from jax.experimental.pallas import tpu as pltpu
from jax.sharding import PartitionSpec as P

HEADS = 16
ABSENT = 100.0
F32 = jnp.float32
BF16 = jnp.bfloat16
VMEM_LIMIT = 40 * 1024 * 1024


def cost(flops, bytes_accessed, transcendentals=0):
    return pl.CostEstimate(
        flops=flops, bytes_accessed=bytes_accessed, transcendentals=transcendentals
    )


def params():
    return pltpu.CompilerParams(vmem_limit_bytes=VMEM_LIMIT)


def dot_nt(a, b):
    return lax.dot_general(a, b, (((1,), (1,)), ((), ())), preferred_element_type=F32)


def dot_nn(a, b):
    return lax.dot_general(a, b, (((1,), (0,)), ((), ())), preferred_element_type=F32)


def pack_kernel(quarters, lengths_ref, qkv_ref, out_ref):
    rows = qkv_ref.shape[1]
    wide = out_ref.shape[3]
    step = pl.program_id(0)
    for block in range(rows // 16):
        times = step * rows + block * 16 + lax.broadcasted_iota(jnp.int32, (16, wide), 0)
        live = times < lengths_ref[0]
        for quarter in range(quarters):
            for kind in range(3):
                start = (kind * quarters + quarter) * wide
                piece = qkv_ref[0, block * 16 : block * 16 + 16, start : start + wide]
                if kind == 1:
                    piece = jnp.where(live, piece.astype(F32), ABSENT).astype(BF16)
                out_ref[block * quarters + quarter, kind] = piece


def pack(lengths, qkv, quarters):
    _, steps, triple = qkv.shape
    wide = triple // 3 // quarters
    rows = 32
    return pl.pallas_call(
        functools.partial(pack_kernel, quarters),
        grid=(steps // rows,),
        in_specs=[
            pl.BlockSpec(memory_space=pltpu.SMEM),
            pl.BlockSpec((1, rows, triple), lambda i: (0, i, 0)),
        ],
        out_specs=pl.BlockSpec((rows // 16 * quarters, 3, 16, wide), lambda i: (i, 0, 0, 0)),
        out_shape=jax.ShapeDtypeStruct((steps // 16 * quarters, 3, 16, wide), BF16),
        compiler_params=params(),
        cost_estimate=cost(0, 4 * steps * triple),
        name="pack_qkv",
    )(lengths, qkv)


def attend_kernel(head_size, scale, in_ref, out_ref):
    series, _, times, wide = in_ref.shape
    pairs = series * times
    chunk = 128
    for head in range(wide // head_size):
        lanes = slice(head * head_size, (head + 1) * head_size)
        keys = in_ref[:, 1, :, lanes].reshape(pairs, head_size)
        values = in_ref[:, 2, :, lanes].reshape(pairs, head_size)
        total = dot_nt(jnp.ones((8, head_size), BF16), keys)[0:1]
        live = total < 0.5 * ABSENT * head_size
        for part in range(pairs // chunk):
            first = part * chunk // times
            count = chunk // times
            queries = in_ref[first : first + count, 0, :, lanes].reshape(chunk, head_size)
            scores = dot_nt(queries, keys) * scale
            row = part * chunk + lax.broadcasted_iota(jnp.int32, (chunk, pairs), 0)
            column = lax.broadcasted_iota(jnp.int32, (chunk, pairs), 1)
            allowed = (((row ^ column) & (times - 1)) == 0) & (live | (row == column))
            scores = jnp.where(allowed, scores, -1e30)
            highest = jnp.max(scores, axis=1, keepdims=True)
            raised = jnp.exp(scores - highest)
            weights = (raised / jnp.sum(raised, axis=1, keepdims=True)).astype(BF16)
            attended = dot_nn(weights, values).astype(BF16)
            out_ref[first : first + count, :, lanes] = attended.reshape(count, times, head_size)


def attend(received, head_size):
    series, _, times, wide = received.shape
    pairs = series * times
    heads = wide // head_size
    return pl.pallas_call(
        functools.partial(attend_kernel, head_size, 1.0 / math.sqrt(head_size)),
        out_shape=jax.ShapeDtypeStruct((series, times, wide), BF16),
        compiler_params=params(),
        cost_estimate=cost(
            4 * heads * pairs * pairs * head_size, received.size * 8 // 3, heads * pairs * pairs
        ),
        name="attend",
    )(received)


def route_kernel(capacity, ids_ref, gates_ref, cotangent_ref, put_ref, take_ref, mix_ref, send_ref):
    tokens = ids_ref.shape[1]
    slots = put_ref.shape[0]
    ids = ids_ref[0]
    gates = gates_ref[0].astype(F32)
    lane = lax.broadcasted_iota(jnp.int32, (tokens, tokens), 1)
    sub = lax.broadcasted_iota(jnp.int32, (tokens, tokens), 0)
    named = [(lane == ids[:, k : k + 1]).astype(F32) for k in range(2)]
    earlier = (lane < sub).astype(BF16)
    before = dot_nn(earlier, (named[0] + named[1]).astype(BF16))
    slot = [
        ids[:, k : k + 1].astype(F32) * capacity
        + jnp.sum(before * named[k], axis=1, keepdims=True)
        for k in range(2)
    ]
    flat = [jnp.transpose(jnp.broadcast_to(slot[k], (tokens, tokens)))[0:1] for k in range(2)]
    flat_gate = [
        jnp.transpose(jnp.broadcast_to(gates[:, k : k + 1], (tokens, tokens)))[0:1]
        for k in range(2)
    ]
    along = lax.broadcasted_iota(jnp.int32, (tokens, slots), 1).astype(F32)
    down = lax.broadcasted_iota(jnp.int32, (slots, tokens), 0).astype(F32)
    hit = [along == slot[k] for k in range(2)]
    take_ref[...] = jnp.where(hit[0] | hit[1], 1.0, 0.0).astype(BF16)
    mix_ref[...] = jnp.where(
        hit[0], gates[:, 0:1], jnp.where(hit[1], gates[:, 1:2], 0.0)
    ).astype(BF16)
    fall = [down == flat[k] for k in range(2)]
    put_ref[...] = jnp.where(fall[0] | fall[1], 1.0, 0.0).astype(BF16)
    weigh = jnp.where(fall[0], flat_gate[0], jnp.where(fall[1], flat_gate[1], 0.0)).astype(BF16)
    wide = cotangent_ref.shape[2]
    for start in range(0, wide, 512):
        send_ref[:, start : start + 512] = dot_nn(
            weigh, cotangent_ref[0, :, start : start + 512]
        ).astype(BF16)


def route(ids, gates, cotangent, capacity, slots):
    _, tokens, wide = cotangent.shape
    return pl.pallas_call(
        functools.partial(route_kernel, capacity),
        out_shape=(
            jax.ShapeDtypeStruct((slots, tokens), BF16),
            jax.ShapeDtypeStruct((tokens, slots), BF16),
            jax.ShapeDtypeStruct((tokens, slots), BF16),
            jax.ShapeDtypeStruct((slots, wide), BF16),
        ),
        compiler_params=params(),
        cost_estimate=cost(2 * slots * tokens * wide, 2 * (slots + tokens) * wide),
        name="route",
    )(ids, gates, cotangent)


def norm_kernel(quarters, lengths_ref, att_ref, resid_ref, gain_ref, put_ref, stream_ref, inverse_ref, send_ref):
    blocks, times, wide = att_ref.shape
    for block in range(blocks):
        at, quarter = block // quarters, block % quarters
        rows = slice(at * times, (at + 1) * times)
        lanes = slice(quarter * wide, (quarter + 1) * wide)
        live = at * times + lax.broadcasted_iota(jnp.int32, (times, wide), 0) < lengths_ref[0]
        stream_ref[rows, lanes] = resid_ref[0, rows, lanes].astype(F32) + jnp.where(
            live, att_ref[block].astype(F32), 0.0
        )
    width = stream_ref.shape[1]
    stream = stream_ref[...]
    inverse = 1.0 / jnp.sqrt(jnp.sum(stream * stream, axis=1, keepdims=True) / width + 1e-05)
    inverse_ref[...] = jnp.broadcast_to(inverse, inverse_ref.shape)
    for start in range(0, width, 512):
        lanes = slice(start, start + 512)
        normed = (stream_ref[:, lanes] * inverse * gain_ref[:, lanes]).astype(BF16)
        send_ref[:, lanes] = dot_nn(put_ref[...], normed).astype(BF16)


def norm(lengths, att, resid, gain, put, quarters):
    _, tokens, width = resid.shape
    slots = put.shape[0]
    vmem = pl.BlockSpec(memory_space=pltpu.VMEM)
    return pl.pallas_call(
        functools.partial(norm_kernel, quarters),
        in_specs=[pl.BlockSpec(memory_space=pltpu.SMEM), vmem, vmem, vmem, vmem],
        out_shape=(
            jax.ShapeDtypeStruct((tokens, width), F32),
            jax.ShapeDtypeStruct((tokens, 128), F32),
            jax.ShapeDtypeStruct((slots, width), BF16),
        ),
        compiler_params=params(),
        cost_estimate=cost(2 * slots * tokens * width, 2 * (slots + 4 * tokens) * width),
        name="norm",
    )(lengths, att, resid, gain, put)


def expert_kernel(x_ref, gh_ref, gate_ref, up_ref, down_ref, out_ref, hidden_ref, gg_ref, gu_ref, acc_ref):
    step = pl.program_id(0)
    gate_pre = dot_nt(x_ref[...], gate_ref[0])
    up_pre = dot_nt(x_ref[...], up_ref[0])
    sigmoid = 1.0 / (1.0 + jnp.exp(-gate_pre))
    silu = gate_pre * sigmoid
    hidden = (silu * up_pre).astype(BF16)
    hidden_ref[...] = hidden
    product = dot_nn(hidden, down_ref[0])

    @pl.when(step == 0)
    def _():
        acc_ref[...] = product

    @pl.when((step > 0) & (step < pl.num_programs(0) - 1))
    def _():
        acc_ref[...] += product

    @pl.when(step == pl.num_programs(0) - 1)
    def _():
        out_ref[...] = (acc_ref[...] + product).astype(BF16)

    grad_hidden = gh_ref[...]
    gg_ref[...] = (grad_hidden * up_pre * sigmoid * (1.0 + gate_pre * (1.0 - sigmoid))).astype(BF16)
    gu_ref[...] = (grad_hidden * silu).astype(BF16)


def expert(x, grad_hidden, gate, up, down):
    rows, width = x.shape
    units = gate.shape[1]
    block = 256
    weight = pl.BlockSpec((1, block, width), lambda i: (0, i, 0))
    column = pl.BlockSpec((rows, block), lambda i: (0, i))
    whole = pl.BlockSpec((rows, width), lambda i: (0, 0))
    return pl.pallas_call(
        expert_kernel,
        grid=(units // block,),
        in_specs=[whole, column, weight, weight, weight],
        out_specs=(whole, column, column, column),
        out_shape=(
            jax.ShapeDtypeStruct((rows, width), BF16),
            jax.ShapeDtypeStruct((rows, units), BF16),
            jax.ShapeDtypeStruct((rows, units), BF16),
            jax.ShapeDtypeStruct((rows, units), BF16),
        ),
        scratch_shapes=[pltpu.VMEM((rows, width), F32)],
        compiler_params=pltpu.CompilerParams(
            dimension_semantics=("arbitrary",), vmem_limit_bytes=VMEM_LIMIT
        ),
        cost_estimate=cost(
            6 * rows * width * units, 4 * rows * width + 6 * units * width, rows * units
        ),
        name="expert",
    )(x, grad_hidden, gate, up, down)


def finish_kernel(take_ref, home_ref, stream_ref, inverse_ref, gain_ref, out_ref):
    width = stream_ref.shape[1]
    inverse = inverse_ref[:, 0:1]
    total = 0.0
    for start in range(0, width, 512):
        lanes = slice(start, start + 512)
        scaled = dot_nn(take_ref[...], home_ref[:, lanes]) * gain_ref[:, lanes]
        out_ref[0, :, lanes] = scaled
        total = total + jnp.sum(stream_ref[:, lanes] * scaled, axis=1, keepdims=True)
    factor = inverse * inverse * inverse * (total / width)
    out_ref[0] = inverse * out_ref[0] - stream_ref[...] * factor


def finish(take, home, stream, inverse, gain):
    tokens, width = stream.shape
    slots = home.shape[0]
    return pl.pallas_call(
        finish_kernel,
        out_shape=jax.ShapeDtypeStruct((1, tokens, width), F32),
        compiler_params=params(),
        cost_estimate=cost(2 * slots * tokens * width, 2 * (slots + 4 * tokens) * width),
        name="finish",
    )(take, home, stream, inverse, gain)


def swap(values, axis="expert"):
    return lax.all_to_all(values, axis, split_axis=0, concat_axis=0, tiled=True)


def body(qkv, resid, lengths, norm_gain, expert_ids, gate_vals, w_gate, w_up, w_down, cotangent):
    _, steps, triple = qkv.shape
    width = triple // 3
    head_size = width // HEADS
    owners = lax.axis_size("expert")
    quarters = owners // (steps // 16)
    capacity = 2 * steps * expert_ids.shape[2] // owners
    slots = owners * capacity
    gain = norm_gain.reshape(1, width)

    down_full = lax.all_gather(w_down, "dp", axis=2, tiled=True)
    gate_full = lax.all_gather(w_gate, "dp", axis=2, tiled=True)
    up_full = lax.all_gather(w_up, "dp", axis=2, tiled=True)

    received = swap(pack(lengths, qkv, quarters))
    put, take, mix, adjoint_send = route(expert_ids, gate_vals, cotangent, capacity, slots)
    grad_out = swap(adjoint_send.reshape(owners, capacity, width)).reshape(slots, width)
    att_home = swap(attend(received, head_size))
    stream, inverse, normed_send = norm(lengths, att_home, resid, gain, put, quarters)
    x_rows = swap(normed_send.reshape(owners, capacity, width)).reshape(slots, width)

    grad_hidden = dot_nt(grad_out, down_full[0])
    expert_out, hidden, grad_gate_pre, grad_up_pre = expert(
        x_rows, grad_hidden, gate_full, up_full, down_full
    )
    out_home = swap(expert_out.reshape(owners, capacity, width)).reshape(slots, width)

    def weight_grad(left, right):
        part = lax.dot_general(left, right, (((0,), (0,)), ((), ())), preferred_element_type=F32)
        return lax.psum_scatter(
            part.astype(BF16)[None], "dp", scatter_dimension=2, tiled=True
        ).astype(F32)

    grad_gate = weight_grad(grad_gate_pre, x_rows)
    grad_up = weight_grad(grad_up_pre, x_rows)
    grad_down = weight_grad(hidden, grad_out)
    grad_rows = (dot_nn(grad_gate_pre, gate_full[0]) + dot_nn(grad_up_pre, up_full[0])).astype(BF16)
    grad_home = swap(grad_rows.reshape(owners, capacity, width)).reshape(slots, width)

    mixture = dot_nn(mix, out_home).astype(BF16)[None]
    grad_stream = finish(take, grad_home, stream, inverse, gain)
    return (mixture, grad_stream, grad_gate, grad_up, grad_down)


def solution(mesh):
    tokens = P(("dp", "expert"), None, None)
    weights = P("expert", None, "dp")
    in_specs = (
        tokens,
        tokens,
        P(("dp", "expert")),
        P(),
        tokens,
        tokens,
        weights,
        weights,
        weights,
        tokens,
    )
    out_specs = (tokens, tokens, weights, weights, weights)
    return jax.shard_map(body, mesh=mesh, in_specs=in_specs, out_specs=out_specs, check_vma=False)
```

```python
import functools
import math

import jax
import jax.numpy as jnp
from jax import lax
from jax.experimental import pallas as pl
from jax.experimental.pallas import tpu as pltpu
from jax.sharding import PartitionSpec as P

HEADS = 16
ABSENT = 100.0
F32 = jnp.float32
BF16 = jnp.bfloat16
VMEM_LIMIT = 40 * 1024 * 1024


def cost(flops, bytes_accessed, transcendentals=0):
    return pl.CostEstimate(
        flops=flops, bytes_accessed=bytes_accessed, transcendentals=transcendentals
    )


def params():
    return pltpu.CompilerParams(vmem_limit_bytes=VMEM_LIMIT)


def dot_nt(a, b):
    return lax.dot_general(a, b, (((1,), (1,)), ((), ())), preferred_element_type=F32)


def flat_rows(ref):
    return ref[...].reshape(ref.shape[0] * ref.shape[1], ref.shape[2])


def dot_nn(a, b):
    return lax.dot_general(a, b, (((1,), (0,)), ((), ())), preferred_element_type=F32)


def pack_kernel(quarters, lengths_ref, qkv_ref, out_ref):
    rows = qkv_ref.shape[1]
    wide = out_ref.shape[3]
    step = pl.program_id(0)
    for block in range(rows // 16):
        times = step * rows + block * 16 + lax.broadcasted_iota(jnp.int32, (16, wide), 0)
        live = times < lengths_ref[0]
        for quarter in range(quarters):
            for kind in range(3):
                start = (kind * quarters + quarter) * wide
                piece = qkv_ref[0, block * 16 : block * 16 + 16, start : start + wide]
                if kind == 1:
                    piece = jnp.where(live, piece.astype(F32), ABSENT).astype(BF16)
                out_ref[block * quarters + quarter, kind] = piece


def pack(lengths, qkv, quarters):
    _, steps, triple = qkv.shape
    wide = triple // 3 // quarters
    rows = 32
    return pl.pallas_call(
        functools.partial(pack_kernel, quarters),
        grid=(steps // rows,),
        in_specs=[
            pl.BlockSpec(memory_space=pltpu.SMEM),
            pl.BlockSpec((1, rows, triple), lambda i: (0, i, 0)),
        ],
        out_specs=pl.BlockSpec((rows // 16 * quarters, 3, 16, wide), lambda i: (i, 0, 0, 0)),
        out_shape=jax.ShapeDtypeStruct((steps // 16 * quarters, 3, 16, wide), BF16),
        compiler_params=params(),
        cost_estimate=cost(0, 4 * steps * triple),
        name="pack_qkv",
    )(lengths, qkv)


def attend_kernel(head_size, scale, in_ref, shared_ref, out_ref):
    del shared_ref
    series, _, times, wide = in_ref.shape
    pairs = series * times
    chunk = 128
    for head in range(wide // head_size):
        lanes = slice(head * head_size, (head + 1) * head_size)
        keys = in_ref[:, 1, :, lanes].reshape(pairs, head_size)
        values = in_ref[:, 2, :, lanes].reshape(pairs, head_size)
        total = dot_nt(jnp.ones((8, head_size), BF16), keys)[0:1]
        live = total < 0.5 * ABSENT * head_size
        for part in range(pairs // chunk):
            first = part * chunk // times
            count = chunk // times
            queries = in_ref[first : first + count, 0, :, lanes].reshape(chunk, head_size)
            scores = dot_nt(queries, keys) * scale
            row = part * chunk + lax.broadcasted_iota(jnp.int32, (chunk, pairs), 0)
            column = lax.broadcasted_iota(jnp.int32, (chunk, pairs), 1)
            allowed = (((row ^ column) & (times - 1)) == 0) & (live | (row == column))
            scores = jnp.where(allowed, scores, -1e30)
            highest = jnp.max(scores, axis=1, keepdims=True)
            raised = jnp.exp(scores - highest)
            weights = (raised / jnp.sum(raised, axis=1, keepdims=True)).astype(BF16)
            attended = dot_nn(weights, values).astype(BF16)
            out_ref[first : first + count, :, lanes] = attended.reshape(count, times, head_size)


def attend(received, shared, head_size):
    series, _, times, wide = received.shape
    pairs = series * times
    heads = wide // head_size
    last = shared.shape[2] // wide - 1
    return pl.pallas_call(
        functools.partial(attend_kernel, head_size, 1.0 / math.sqrt(head_size)),
        grid=(1,),
        in_specs=[
            pl.BlockSpec(received.shape, lambda i: (0, 0, 0, 0)),
            pl.BlockSpec(memory_space=pl.ANY),
        ],
        out_specs=pl.BlockSpec((series, times, wide), lambda i: (0, 0, last)),
        out_shape=jax.ShapeDtypeStruct(shared.shape, BF16),
        input_output_aliases={1: 0},
        compiler_params=params(),
        cost_estimate=cost(
            4 * heads * pairs * pairs * head_size, received.size * 8 // 3, heads * pairs * pairs
        ),
        name="attend",
    )(received, shared)


def route_kernel(capacity, ids_ref, gates_ref, cotangent_ref, put_ref, take_ref, mix_ref, send_ref):
    tokens = ids_ref.shape[1]
    slots = put_ref.shape[0]
    ids = ids_ref[0]
    gates = gates_ref[0].astype(F32)
    lane = lax.broadcasted_iota(jnp.int32, (tokens, tokens), 1)
    sub = lax.broadcasted_iota(jnp.int32, (tokens, tokens), 0)
    named = [(lane == ids[:, k : k + 1]).astype(F32) for k in range(2)]
    earlier = (lane < sub).astype(BF16)
    before = dot_nn(earlier, (named[0] + named[1]).astype(BF16))
    slot = [
        ids[:, k : k + 1].astype(F32) * capacity
        + jnp.sum(before * named[k], axis=1, keepdims=True)
        for k in range(2)
    ]
    flat = [jnp.transpose(jnp.broadcast_to(slot[k], (tokens, tokens)))[0:1] for k in range(2)]
    flat_gate = [
        jnp.transpose(jnp.broadcast_to(gates[:, k : k + 1], (tokens, tokens)))[0:1]
        for k in range(2)
    ]
    along = lax.broadcasted_iota(jnp.int32, (tokens, slots), 1).astype(F32)
    down = lax.broadcasted_iota(jnp.int32, (slots, tokens), 0).astype(F32)
    hit = [along == slot[k] for k in range(2)]
    take_ref[...] = jnp.where(hit[0] | hit[1], 1.0, 0.0).astype(BF16)
    mix_ref[...] = jnp.where(
        hit[0], gates[:, 0:1], jnp.where(hit[1], gates[:, 1:2], 0.0)
    ).astype(BF16)
    fall = [down == flat[k] for k in range(2)]
    put_ref[...] = jnp.where(fall[0] | fall[1], 1.0, 0.0).astype(BF16)
    weigh = jnp.where(fall[0], flat_gate[0], jnp.where(fall[1], flat_gate[1], 0.0)).astype(BF16)
    owners = slots // capacity
    wide = cotangent_ref.shape[2]
    for start in range(0, wide, 512):
        rows = dot_nn(weigh, cotangent_ref[0, :, start : start + 512]).astype(BF16)
        send_ref[:, :, start : start + 512] = rows.reshape(owners, capacity, 512)


def route(ids, gates, cotangent, capacity, slots, extra):
    _, tokens, wide = cotangent.shape
    return pl.pallas_call(
        functools.partial(route_kernel, capacity),
        out_shape=(
            jax.ShapeDtypeStruct((slots, tokens), BF16),
            jax.ShapeDtypeStruct((tokens, slots), BF16),
            jax.ShapeDtypeStruct((tokens, slots), BF16),
            jax.ShapeDtypeStruct((slots // capacity, capacity, wide + extra), BF16),
        ),
        grid=(1,),
        in_specs=[
            pl.BlockSpec(ids.shape, lambda i: (0, 0, 0)),
            pl.BlockSpec(gates.shape, lambda i: (0, 0, 0)),
            pl.BlockSpec(cotangent.shape, lambda i: (0, 0, 0)),
        ],
        out_specs=(
            pl.BlockSpec((slots, tokens), lambda i: (0, 0)),
            pl.BlockSpec((tokens, slots), lambda i: (0, 0)),
            pl.BlockSpec((tokens, slots), lambda i: (0, 0)),
            pl.BlockSpec((slots // capacity, capacity, wide), lambda i: (0, 0, 0)),
        ),
        compiler_params=params(),
        cost_estimate=cost(2 * slots * tokens * wide, 2 * (slots + tokens) * wide),
        name="route",
    )(ids, gates, cotangent)


def norm_kernel(quarters, lengths_ref, att_ref, resid_ref, gain_ref, put_ref, stream_ref, inverse_ref, send_ref):
    blocks, times, wide = att_ref.shape
    for block in range(blocks):
        at, quarter = block // quarters, block % quarters
        rows = slice(at * times, (at + 1) * times)
        lanes = slice(quarter * wide, (quarter + 1) * wide)
        live = at * times + lax.broadcasted_iota(jnp.int32, (times, wide), 0) < lengths_ref[0]
        stream_ref[rows, lanes] = resid_ref[0, rows, lanes].astype(F32) + jnp.where(
            live, att_ref[block].astype(F32), 0.0
        )
    width = stream_ref.shape[1]
    stream = stream_ref[...]
    inverse = 1.0 / jnp.sqrt(jnp.sum(stream * stream, axis=1, keepdims=True) / width + 1e-05)
    inverse_ref[...] = jnp.broadcast_to(inverse, inverse_ref.shape)
    for start in range(0, width, 512):
        lanes = slice(start, start + 512)
        normed = (stream_ref[:, lanes] * inverse * gain_ref[:, lanes]).astype(BF16)
        rows = dot_nn(put_ref[...], normed).astype(BF16)
        send_ref[:, :, lanes] = rows.reshape(send_ref.shape[0], send_ref.shape[1], 512)


def norm(lengths, att, resid, gain, put, quarters):
    _, tokens, width = resid.shape
    slots = put.shape[0]
    blocks, times, whole = att.shape
    wide = width // quarters
    return pl.pallas_call(
        functools.partial(norm_kernel, quarters),
        grid=(1,),
        in_specs=[
            pl.BlockSpec(memory_space=pltpu.SMEM),
            pl.BlockSpec((blocks, times, wide), lambda i: (0, 0, whole // wide - 1)),
            pl.BlockSpec(resid.shape, lambda i: (0, 0, 0)),
            pl.BlockSpec(gain.shape, lambda i: (0, 0)),
            pl.BlockSpec(put.shape, lambda i: (0, 0)),
        ],
        out_specs=(
            pl.BlockSpec((tokens, width), lambda i: (0, 0)),
            pl.BlockSpec((tokens, 128), lambda i: (0, 0)),
            pl.BlockSpec((blocks, slots // blocks, width), lambda i: (0, 0, 0)),
        ),
        out_shape=(
            jax.ShapeDtypeStruct((tokens, width), F32),
            jax.ShapeDtypeStruct((tokens, 128), F32),
            jax.ShapeDtypeStruct((blocks, slots // blocks, width), BF16),
        ),
        compiler_params=params(),
        cost_estimate=cost(2 * slots * tokens * width, 2 * (slots + 4 * tokens) * width),
        name="norm",
    )(lengths, att, resid, gain, put)


def expert_kernel(x_ref, gh_ref, gate_ref, up_ref, down_ref, out_ref, inner_ref, acc_ref):
    step = pl.program_id(0)
    x = flat_rows(x_ref)
    gate_pre = dot_nt(x, gate_ref[0])
    up_pre = dot_nt(x, up_ref[0])
    sigmoid = 1.0 / (1.0 + jnp.exp(-gate_pre))
    silu = gate_pre * sigmoid
    hidden = (silu * up_pre).astype(BF16)
    inner_ref[2] = hidden
    product = dot_nn(hidden, down_ref[0])

    @pl.when(step == 0)
    def _():
        acc_ref[...] = product

    @pl.when((step > 0) & (step < pl.num_programs(0) - 1))
    def _():
        acc_ref[...] += product

    @pl.when(step == pl.num_programs(0) - 1)
    def _():
        out_ref[...] = (acc_ref[...] + product).astype(BF16).reshape(out_ref.shape)

    grad_hidden = gh_ref[...]
    inner_ref[0] = (
        grad_hidden * up_pre * sigmoid * (1.0 + gate_pre * (1.0 - sigmoid))
    ).astype(BF16)
    inner_ref[1] = (grad_hidden * silu).astype(BF16)


def expert(x, grad_hidden, gate, up, down):
    owners, capacity, width = x.shape
    rows = owners * capacity
    units = gate.shape[1]
    block = 256
    weight = pl.BlockSpec((1, block, width), lambda i: (0, i, 0))
    column = pl.BlockSpec((rows, block), lambda i: (0, i))
    whole = pl.BlockSpec((owners, capacity, width), lambda i: (0, 0, 0))
    return pl.pallas_call(
        expert_kernel,
        grid=(units // block,),
        in_specs=[whole, column, weight, weight, weight],
        out_specs=(whole, pl.BlockSpec((3, rows, block), lambda i: (0, 0, i))),
        out_shape=(
            jax.ShapeDtypeStruct(x.shape, BF16),
            jax.ShapeDtypeStruct((3, rows, units), BF16),
        ),
        scratch_shapes=[pltpu.VMEM((rows, width), F32)],
        compiler_params=pltpu.CompilerParams(
            dimension_semantics=("arbitrary",), vmem_limit_bytes=VMEM_LIMIT
        ),
        cost_estimate=cost(
            6 * rows * width * units, 4 * rows * width + 6 * units * width, rows * units
        ),
        name="expert",
    )(x, grad_hidden, gate, up, down)


def grad_hidden_kernel(grad_out_ref, down_ref, out_ref):
    out_ref[...] = dot_nt(flat_rows(grad_out_ref), down_ref[0])


def hidden_grad(shared, down):
    owners, capacity, _ = shared.shape
    rows = owners * capacity
    _, units, width = down.shape
    block = 256
    return pl.pallas_call(
        grad_hidden_kernel,
        grid=(units // block,),
        in_specs=[
            pl.BlockSpec((owners, capacity, width), lambda i: (0, 0, 0)),
            pl.BlockSpec((1, block, width), lambda i: (0, i, 0)),
        ],
        out_specs=pl.BlockSpec((rows, block), lambda i: (0, i)),
        out_shape=jax.ShapeDtypeStruct((rows, units), F32),
        compiler_params=params(),
        cost_estimate=cost(2 * rows * units * width, 2 * width * (rows + units) + 4 * rows * units),
        name="grad_hidden",
    )(shared, down)


def rows_kernel(inner_ref, gate_ref, up_ref, out_ref, acc_ref):
    step = pl.program_id(0)
    product = dot_nn(inner_ref[0], gate_ref[0]) + dot_nn(inner_ref[1], up_ref[0])

    @pl.when(step == 0)
    def _():
        acc_ref[...] = product

    @pl.when((step > 0) & (step < pl.num_programs(0) - 1))
    def _():
        acc_ref[...] += product

    @pl.when(step == pl.num_programs(0) - 1)
    def _():
        out_ref[...] = (acc_ref[...] + product).astype(BF16).reshape(out_ref.shape)


def row_grads(inner, gate, up, capacity):
    _, rows, units = inner.shape
    width = gate.shape[2]
    block = 256
    weight = pl.BlockSpec((1, block, width), lambda i: (0, i, 0))
    shape = (rows // capacity, capacity, width)
    return pl.pallas_call(
        rows_kernel,
        grid=(units // block,),
        in_specs=[pl.BlockSpec((2, rows, block), lambda i: (0, 0, i)), weight, weight],
        out_specs=pl.BlockSpec(shape, lambda i: (0, 0, 0)),
        out_shape=jax.ShapeDtypeStruct(shape, BF16),
        scratch_shapes=[pltpu.VMEM((rows, width), F32)],
        compiler_params=params(),
        cost_estimate=cost(
            4 * rows * units * width, 4 * units * width + 2 * rows * (width + 2 * units)
        ),
        name="grad_rows",
    )(inner, gate, up)


def mix_kernel(mix_ref, home_ref, out_ref):
    for start in range(0, home_ref.shape[2], 512):
        lanes = slice(start, start + 512)
        home = home_ref[:, :, lanes].reshape(mix_ref.shape[1], 512)
        out_ref[0, :, lanes] = dot_nn(mix_ref[...], home).astype(BF16)


def mixed(mix, home):
    tokens, slots = mix.shape
    width = home.shape[2]
    return pl.pallas_call(
        mix_kernel,
        out_shape=jax.ShapeDtypeStruct((1, tokens, width), BF16),
        compiler_params=params(),
        cost_estimate=cost(2 * slots * tokens * width, 2 * (slots + tokens) * width),
        name="mixture",
    )(mix, home)


def partial_kernel(inner_ref, x_ref, grad_out_ref, out_ref):
    def product(right):
        return lax.dot_general(
            inner_ref[0], right, (((0,), (0,)), ((), ())), preferred_element_type=F32
        ).astype(BF16)

    @pl.when(pl.program_id(0) < 2)
    def _():
        out_ref[...] = product(flat_rows(x_ref))

    @pl.when(pl.program_id(0) == 2)
    def _():
        out_ref[...] = product(flat_rows(grad_out_ref))


def partials(inner, x, shared):
    kinds, rows, units = inner.shape
    width = x.shape[2]
    block = 256
    count = units // block
    whole = pl.BlockSpec(x.shape, lambda k, i: (0, 0, 0))
    return pl.pallas_call(
        partial_kernel,
        grid=(kinds, count),
        in_specs=[pl.BlockSpec((1, rows, block), lambda k, i: (k, 0, i)), whole, whole],
        out_specs=pl.BlockSpec((block, width), lambda k, i: (k * count + i, 0)),
        out_shape=jax.ShapeDtypeStruct((kinds * units, width), BF16),
        compiler_params=pltpu.CompilerParams(vmem_limit_bytes=58 * 1024 * 1024),
        cost_estimate=cost(2 * kinds * rows * units * width, 4 * (kinds * units + rows) * width),
        name="partials",
    )(inner, x, shared)


def widen_kernel(in_ref, *out_refs):
    units = out_refs[0].shape[1]
    for k, out_ref in enumerate(out_refs):
        out_ref[0] = in_ref[k * units : (k + 1) * units].astype(F32)


def widen(grads, units):
    rows, width = grads.shape
    return pl.pallas_call(
        widen_kernel,
        out_shape=(jax.ShapeDtypeStruct((1, units, width), F32),) * (rows // units),
        compiler_params=params(),
        cost_estimate=cost(0, 6 * rows * width),
        name="widen",
    )(grads)


def finish_kernel(take_ref, home_ref, stream_ref, inverse_ref, gain_ref, out_ref):
    width = stream_ref.shape[1]
    inverse = inverse_ref[:, 0:1]
    total = 0.0
    for start in range(0, width, 512):
        lanes = slice(start, start + 512)
        home = home_ref[:, :, lanes].reshape(take_ref.shape[1], 512)
        scaled = dot_nn(take_ref[...], home) * gain_ref[:, lanes]
        out_ref[0, :, lanes] = scaled
        total = total + jnp.sum(stream_ref[:, lanes] * scaled, axis=1, keepdims=True)
    factor = inverse * inverse * inverse * (total / width)
    out_ref[0] = inverse * out_ref[0] - stream_ref[...] * factor


def finish(take, home, stream, inverse, gain):
    tokens, width = stream.shape
    slots = take.shape[1]
    return pl.pallas_call(
        finish_kernel,
        out_shape=jax.ShapeDtypeStruct((1, tokens, width), F32),
        compiler_params=params(),
        cost_estimate=cost(2 * slots * tokens * width, 2 * (slots + 4 * tokens) * width),
        name="finish",
    )(take, home, stream, inverse, gain)


def in_hbm(values):
    return pltpu.with_memory_space_constraint(values, pltpu.HBM)


def swap(values, axis="expert"):
    return lax.all_to_all(values, axis, split_axis=0, concat_axis=0, tiled=True)


def body(qkv, resid, lengths, norm_gain, expert_ids, gate_vals, w_gate, w_up, w_down, cotangent):
    _, steps, triple = qkv.shape
    width = triple // 3
    head_size = width // HEADS
    owners = lax.axis_size("expert")
    quarters = owners // (steps // 16)
    capacity = 2 * steps * expert_ids.shape[2] // owners
    slots = owners * capacity
    gain = norm_gain.reshape(1, width)

    down_full = lax.all_gather(w_down, "dp", axis=2, tiled=True)
    gate_full = lax.all_gather(w_gate, "dp", axis=2, tiled=True)
    up_full = lax.all_gather(w_up, "dp", axis=2, tiled=True)

    received = swap(pack(lengths, qkv, quarters))
    put, take, mix, adjoint_send = route(
        expert_ids, gate_vals, cotangent, capacity, slots, width // quarters
    )
    shared = swap(in_hbm(attend(received, in_hbm(adjoint_send), head_size)))
    stream, inverse, normed_send = norm(lengths, shared, resid, gain, put, quarters)
    x_rows = swap(in_hbm(normed_send))

    gate_full, up_full, down_full = in_hbm(gate_full), in_hbm(up_full), in_hbm(down_full)
    grad_hidden = in_hbm(hidden_grad(shared, down_full))
    expert_out, inner = expert(x_rows, grad_hidden, gate_full, up_full, down_full)
    inner = in_hbm(inner)
    out_home = swap(in_hbm(expert_out))

    grads = lax.psum_scatter(
        partials(inner, x_rows, shared), "dp", scatter_dimension=1, tiled=True
    )
    grad_gate, grad_up, grad_down = widen(grads, w_gate.shape[1])
    grad_rows = in_hbm(row_grads(inner, gate_full, up_full, capacity))
    grad_rows, out_home = lax.optimization_barrier((grad_rows, out_home))
    grad_home = swap(grad_rows)

    mixture = mixed(mix, out_home)
    grad_stream = finish(take, grad_home, stream, inverse, gain)
    return (mixture, grad_stream, grad_gate, grad_up, grad_down)


def solution(mesh):
    tokens = P(("dp", "expert"), None, None)
    weights = P("expert", None, "dp")
    in_specs = (
        tokens,
        tokens,
        P(("dp", "expert")),
        P(),
        tokens,
        tokens,
        weights,
        weights,
        weights,
        tokens,
    )
    out_specs = (tokens, tokens, weights, weights, weights)
    return jax.shard_map(body, mesh=mesh, in_specs=in_specs, out_specs=out_specs, check_vma=False)
```

```python
import functools
import math

import jax
import jax.numpy as jnp
from jax import lax
from jax.experimental import pallas as pl
from jax.experimental.pallas import tpu as pltpu
from jax.sharding import PartitionSpec as P

HEADS = 16
ABSENT = 100.0
F32 = jnp.float32
BF16 = jnp.bfloat16
LONG = 10**15


def cost(flops, bytes_accessed, transcendentals=0):
    return pl.CostEstimate(
        flops=flops, bytes_accessed=bytes_accessed, transcendentals=transcendentals
    )


def params(mebibytes=40):
    return pltpu.CompilerParams(vmem_limit_bytes=mebibytes * 1024 * 1024)


def dot_nt(a, b):
    return lax.dot_general(a, b, (((1,), (1,)), ((), ())), preferred_element_type=F32)


def flat_rows(ref):
    return ref[...].reshape(ref.shape[0] * ref.shape[1], ref.shape[2])


def dot_nn(a, b):
    return lax.dot_general(a, b, (((1,), (0,)), ((), ())), preferred_element_type=F32)


def pack_kernel(quarters, lengths_ref, qkv_ref, out_ref):
    rows = qkv_ref.shape[1]
    wide = out_ref.shape[3]
    step = pl.program_id(0)
    for block in range(rows // 16):
        times = step * rows + block * 16 + lax.broadcasted_iota(jnp.int32, (16, wide), 0)
        live = times < lengths_ref[0]
        for quarter in range(quarters):
            for kind in range(3):
                start = (kind * quarters + quarter) * wide
                piece = qkv_ref[0, block * 16 : block * 16 + 16, start : start + wide]
                if kind == 1:
                    piece = jnp.where(live, piece.astype(F32), ABSENT).astype(BF16)
                out_ref[block * quarters + quarter, kind] = piece


def pack(lengths, qkv, quarters):
    _, steps, triple = qkv.shape
    wide = triple // 3 // quarters
    rows = 32
    return pl.pallas_call(
        functools.partial(pack_kernel, quarters),
        grid=(steps // rows,),
        in_specs=[
            pl.BlockSpec(memory_space=pltpu.SMEM),
            pl.BlockSpec((1, rows, triple), lambda i: (0, i, 0)),
        ],
        out_specs=pl.BlockSpec((rows // 16 * quarters, 3, 16, wide), lambda i: (i, 0, 0, 0)),
        out_shape=jax.ShapeDtypeStruct((steps // 16 * quarters, 3, 16, wide), BF16),
        compiler_params=params(),
        cost_estimate=cost(0, 4 * steps * triple),
        name="pack_qkv",
    )(lengths, qkv)


def attend_kernel(head_size, scale, in_ref, shared_ref, out_ref, bias_ref):
    del shared_ref
    series, _, times, wide = in_ref.shape
    pairs = series * times
    chunk = 128
    keys = in_ref[:, 1, :, 0:head_size].reshape(pairs, head_size)
    total = dot_nt(jnp.ones((8, head_size), BF16), keys)[0:1]
    live = total < 0.5 * ABSENT * head_size
    for part in range(pairs // chunk):
        first = part * chunk // times
        count = chunk // times
        row = part * chunk + lax.broadcasted_iota(jnp.int32, (chunk, pairs), 0)
        column = lax.broadcasted_iota(jnp.int32, (chunk, pairs), 1)
        allowed = (((row ^ column) & (times - 1)) == 0) & (live | (row == column))
        bias_ref[...] = jnp.where(allowed, 0.0, -1e30)
        for head in range(wide // head_size):
            lanes = slice(head * head_size, (head + 1) * head_size)
            queries = in_ref[first : first + count, 0, :, lanes].reshape(chunk, head_size)
            keys = in_ref[:, 1, :, lanes].reshape(pairs, head_size)
            values = in_ref[:, 2, :, lanes].reshape(pairs, head_size)
            scores = dot_nt(queries, keys) * scale + bias_ref[...]
            highest = jnp.max(scores, axis=1, keepdims=True)
            raised = jnp.exp2(scores - highest).astype(BF16)
            both = dot_nn(raised, jnp.concatenate([values, jnp.ones_like(values)], axis=1))
            attended = (both[:, :head_size] / both[:, head_size:]).astype(BF16)
            out_ref[first : first + count, :, lanes] = attended.reshape(count, times, head_size)


def attend(received, shared, head_size):
    series, _, times, wide = received.shape
    pairs = series * times
    heads = wide // head_size
    last = shared.shape[2] // wide - 1
    return pl.pallas_call(
        functools.partial(attend_kernel, head_size, math.log2(math.e) / math.sqrt(head_size)),
        grid=(1,),
        in_specs=[
            pl.BlockSpec(received.shape, lambda i: (0, 0, 0, 0)),
            pl.BlockSpec(memory_space=pl.ANY),
        ],
        out_specs=pl.BlockSpec((series, times, wide), lambda i: (0, 0, last)),
        out_shape=jax.ShapeDtypeStruct(shared.shape, BF16),
        input_output_aliases={1: 0},
        scratch_shapes=[pltpu.VMEM((128, pairs), F32)],
        compiler_params=params(),
        cost_estimate=cost(
            4 * heads * pairs * pairs * head_size, received.size * 8 // 3, heads * pairs * pairs
        ),
        name="attend",
    )(received, shared)


def route_kernel(capacity, ids_ref, gates_ref, cotangent_ref, put_ref, take_ref, mix_ref, send_ref):
    tokens = ids_ref.shape[1]
    slots = put_ref.shape[0]
    ids = ids_ref[0]
    gates = gates_ref[0].astype(F32)
    lane = lax.broadcasted_iota(jnp.int32, (tokens, tokens), 1)
    sub = lax.broadcasted_iota(jnp.int32, (tokens, tokens), 0)
    named = [(lane == ids[:, k : k + 1]).astype(F32) for k in range(2)]
    earlier = (lane < sub).astype(BF16)
    before = dot_nn(earlier, (named[0] + named[1]).astype(BF16))
    slot = [
        ids[:, k : k + 1].astype(F32) * capacity
        + jnp.sum(before * named[k], axis=1, keepdims=True)
        for k in range(2)
    ]
    flat = [jnp.transpose(jnp.broadcast_to(slot[k], (tokens, tokens)))[0:1] for k in range(2)]
    flat_gate = [
        jnp.transpose(jnp.broadcast_to(gates[:, k : k + 1], (tokens, tokens)))[0:1]
        for k in range(2)
    ]
    along = lax.broadcasted_iota(jnp.int32, (tokens, slots), 1).astype(F32)
    down = lax.broadcasted_iota(jnp.int32, (slots, tokens), 0).astype(F32)
    hit = [along == slot[k] for k in range(2)]
    take_ref[...] = jnp.where(hit[0] | hit[1], 1.0, 0.0).astype(BF16)
    mix_ref[...] = jnp.where(
        hit[0], gates[:, 0:1], jnp.where(hit[1], gates[:, 1:2], 0.0)
    ).astype(BF16)
    fall = [down == flat[k] for k in range(2)]
    put_ref[...] = jnp.where(fall[0] | fall[1], 1.0, 0.0).astype(BF16)
    weigh = jnp.where(fall[0], flat_gate[0], jnp.where(fall[1], flat_gate[1], 0.0)).astype(BF16)
    owners = slots // capacity
    wide = cotangent_ref.shape[2]
    for start in range(0, wide, 512):
        rows = dot_nn(weigh, cotangent_ref[0, :, start : start + 512]).astype(BF16)
        send_ref[:, :, start : start + 512] = rows.reshape(owners, capacity, 512)


def route(ids, gates, cotangent, capacity, slots, extra):
    _, tokens, wide = cotangent.shape
    return pl.pallas_call(
        functools.partial(route_kernel, capacity),
        out_shape=(
            jax.ShapeDtypeStruct((slots, tokens), BF16),
            jax.ShapeDtypeStruct((tokens, slots), BF16),
            jax.ShapeDtypeStruct((tokens, slots), BF16),
            jax.ShapeDtypeStruct((slots // capacity, capacity, wide + extra), BF16),
        ),
        grid=(1,),
        in_specs=[
            pl.BlockSpec(ids.shape, lambda i: (0, 0, 0)),
            pl.BlockSpec(gates.shape, lambda i: (0, 0, 0)),
            pl.BlockSpec(cotangent.shape, lambda i: (0, 0, 0)),
        ],
        out_specs=(
            pl.BlockSpec((slots, tokens), lambda i: (0, 0)),
            pl.BlockSpec((tokens, slots), lambda i: (0, 0)),
            pl.BlockSpec((tokens, slots), lambda i: (0, 0)),
            pl.BlockSpec((slots // capacity, capacity, wide), lambda i: (0, 0, 0)),
        ),
        compiler_params=params(),
        cost_estimate=cost(2 * slots * tokens * wide, 2 * (slots + tokens) * wide),
        name="route",
    )(ids, gates, cotangent)


def norm_kernel(quarters, lengths_ref, att_ref, resid_ref, gain_ref, put_ref, stream_ref, inverse_ref, send_ref):
    blocks, times, wide = att_ref.shape
    for block in range(blocks):
        at, quarter = block // quarters, block % quarters
        rows = slice(at * times, (at + 1) * times)
        lanes = slice(quarter * wide, (quarter + 1) * wide)
        live = at * times + lax.broadcasted_iota(jnp.int32, (times, wide), 0) < lengths_ref[0]
        stream_ref[rows, lanes] = resid_ref[0, rows, lanes].astype(F32) + jnp.where(
            live, att_ref[block].astype(F32), 0.0
        )
    width = stream_ref.shape[1]
    stream = stream_ref[...]
    inverse = 1.0 / jnp.sqrt(jnp.sum(stream * stream, axis=1, keepdims=True) / width + 1e-05)
    inverse_ref[...] = jnp.broadcast_to(inverse, inverse_ref.shape)
    for start in range(0, width, 512):
        lanes = slice(start, start + 512)
        normed = (stream_ref[:, lanes] * inverse * gain_ref[:, lanes]).astype(BF16)
        rows = dot_nn(put_ref[...], normed).astype(BF16)
        send_ref[:, :, lanes] = rows.reshape(send_ref.shape[0], send_ref.shape[1], 512)


def norm(lengths, att, resid, gain, put, quarters):
    _, tokens, width = resid.shape
    slots = put.shape[0]
    blocks, times, whole = att.shape
    wide = width // quarters
    return pl.pallas_call(
        functools.partial(norm_kernel, quarters),
        grid=(1,),
        in_specs=[
            pl.BlockSpec(memory_space=pltpu.SMEM),
            pl.BlockSpec((blocks, times, wide), lambda i: (0, 0, whole // wide - 1)),
            pl.BlockSpec(resid.shape, lambda i: (0, 0, 0)),
            pl.BlockSpec(gain.shape, lambda i: (0, 0)),
            pl.BlockSpec(put.shape, lambda i: (0, 0)),
        ],
        out_specs=(
            pl.BlockSpec((tokens, width), lambda i: (0, 0)),
            pl.BlockSpec((tokens, 128), lambda i: (0, 0)),
            pl.BlockSpec((blocks, slots // blocks, width), lambda i: (0, 0, 0)),
        ),
        out_shape=(
            jax.ShapeDtypeStruct((tokens, width), F32),
            jax.ShapeDtypeStruct((tokens, 128), F32),
            jax.ShapeDtypeStruct((blocks, slots // blocks, width), BF16),
        ),
        compiler_params=params(),
        cost_estimate=cost(2 * slots * tokens * width, 2 * (slots + 4 * tokens) * width),
        name="norm",
    )(lengths, att, resid, gain, put)


def expert_kernel(x_ref, gh_ref, gate_ref, up_ref, down_ref, out_ref, inner_ref, acc_ref):
    step = pl.program_id(0)
    x = flat_rows(x_ref)
    gate_pre = dot_nt(x, gate_ref[0])
    up_pre = dot_nt(x, up_ref[0])
    sigmoid = 1.0 / (1.0 + jnp.exp(-gate_pre))
    silu = gate_pre * sigmoid
    hidden = (silu * up_pre).astype(BF16)
    inner_ref[2] = hidden
    product = dot_nn(hidden, down_ref[0])

    @pl.when(step == 0)
    def _():
        acc_ref[...] = product

    @pl.when((step > 0) & (step < pl.num_programs(0) - 1))
    def _():
        acc_ref[...] += product

    @pl.when(step == pl.num_programs(0) - 1)
    def _():
        out_ref[...] = (acc_ref[...] + product).astype(BF16).reshape(out_ref.shape)

    grad_hidden = gh_ref[...]
    inner_ref[0] = (
        grad_hidden * up_pre * sigmoid * (1.0 + gate_pre * (1.0 - sigmoid))
    ).astype(BF16)
    inner_ref[1] = (grad_hidden * silu).astype(BF16)


def expert(x, grad_hidden, gate, up, down):
    owners, capacity, width = x.shape
    rows = owners * capacity
    units = gate.shape[1]
    block = 256
    weight = pl.BlockSpec((1, block, width), lambda i: (0, i, 0))
    column = pl.BlockSpec((rows, block), lambda i: (0, i))
    whole = pl.BlockSpec((owners, capacity, width), lambda i: (0, 0, 0))
    return pl.pallas_call(
        expert_kernel,
        grid=(units // block,),
        in_specs=[whole, column, weight, weight, weight],
        out_specs=(whole, pl.BlockSpec((3, rows, block), lambda i: (0, 0, i))),
        out_shape=(
            jax.ShapeDtypeStruct(x.shape, BF16),
            jax.ShapeDtypeStruct((3, rows, units), BF16),
        ),
        scratch_shapes=[pltpu.VMEM((rows, width), F32)],
        compiler_params=params(60),
        cost_estimate=cost(
            6 * rows * width * units, 4 * rows * width + 6 * units * width, rows * units
        ),
        name="expert",
    )(x, grad_hidden, gate, up, down)


def grad_hidden_kernel(grad_out_ref, down_ref, out_ref):
    out_ref[...] = dot_nt(flat_rows(grad_out_ref), down_ref[0])


def hidden_grad(shared, down):
    owners, capacity, _ = shared.shape
    rows = owners * capacity
    _, units, width = down.shape
    block = 256
    return pl.pallas_call(
        grad_hidden_kernel,
        grid=(units // block,),
        in_specs=[
            pl.BlockSpec((owners, capacity, width), lambda i: (0, 0, 0)),
            pl.BlockSpec((1, block, width), lambda i: (0, i, 0)),
        ],
        out_specs=pl.BlockSpec((rows, block), lambda i: (0, i)),
        out_shape=jax.ShapeDtypeStruct((rows, units), F32),
        compiler_params=params(),
        cost_estimate=cost(2 * rows * units * width, 2 * width * (rows + units) + 4 * rows * units),
        name="grad_hidden",
    )(shared, down)


def rows_kernel(inner_ref, gate_ref, up_ref, out_ref, acc_ref):
    step = pl.program_id(0)
    product = dot_nn(inner_ref[0], gate_ref[0]) + dot_nn(inner_ref[1], up_ref[0])

    @pl.when(step == 0)
    def _():
        acc_ref[...] = product

    @pl.when((step > 0) & (step < pl.num_programs(0) - 1))
    def _():
        acc_ref[...] += product

    @pl.when(step == pl.num_programs(0) - 1)
    def _():
        out_ref[...] = (acc_ref[...] + product).astype(BF16).reshape(out_ref.shape)


def row_grads(inner, gate, up, capacity):
    _, rows, units = inner.shape
    width = gate.shape[2]
    block = 256
    weight = pl.BlockSpec((1, block, width), lambda i: (0, i, 0))
    shape = (rows // capacity, capacity, width)
    return pl.pallas_call(
        rows_kernel,
        grid=(units // block,),
        in_specs=[pl.BlockSpec((2, rows, block), lambda i: (0, 0, i)), weight, weight],
        out_specs=pl.BlockSpec(shape, lambda i: (0, 0, 0)),
        out_shape=jax.ShapeDtypeStruct(shape, BF16),
        scratch_shapes=[pltpu.VMEM((rows, width), F32)],
        compiler_params=params(),
        cost_estimate=cost(
            4 * rows * units * width, 4 * units * width + 2 * rows * (width + 2 * units)
        ),
        name="grad_rows",
    )(inner, gate, up)


def mix_kernel(mix_ref, home_ref, out_ref):
    for start in range(0, home_ref.shape[2], 512):
        lanes = slice(start, start + 512)
        home = home_ref[:, :, lanes].reshape(mix_ref.shape[1], 512)
        out_ref[0, :, lanes] = dot_nn(mix_ref[...], home).astype(BF16)


def mixed(mix, home):
    tokens, slots = mix.shape
    width = home.shape[2]
    return pl.pallas_call(
        mix_kernel,
        out_shape=jax.ShapeDtypeStruct((1, tokens, width), BF16),
        compiler_params=params(),
        cost_estimate=cost(LONG, LONG // 1000),
        name="mixture",
    )(mix, home)


def partial_kernel(inner_ref, x_ref, grad_out_ref, out_ref):
    def product(right):
        return lax.dot_general(
            inner_ref[0], right, (((0,), (0,)), ((), ())), preferred_element_type=F32
        ).astype(BF16)

    @pl.when(pl.program_id(0) < 2)
    def _():
        out_ref[...] = product(flat_rows(x_ref))

    @pl.when(pl.program_id(0) == 2)
    def _():
        out_ref[...] = product(flat_rows(grad_out_ref))


def partials(inner, x, shared):
    kinds, rows, units = inner.shape
    width = x.shape[2]
    block = 256
    count = units // block
    whole = pl.BlockSpec(x.shape, lambda k, i: (0, 0, 0))
    return pl.pallas_call(
        partial_kernel,
        grid=(kinds, count),
        in_specs=[pl.BlockSpec((1, rows, block), lambda k, i: (k, 0, i)), whole, whole],
        out_specs=pl.BlockSpec((block, width), lambda k, i: (k * count + i, 0)),
        out_shape=jax.ShapeDtypeStruct((kinds * units, width), BF16),
        compiler_params=params(58),
        cost_estimate=cost(2 * kinds * rows * units * width, 4 * (kinds * units + rows) * width),
        name="partials",
    )(inner, x, shared)


def widen_kernel(in_ref, *out_refs):
    units = out_refs[0].shape[1]
    for k, out_ref in enumerate(out_refs):
        out_ref[0] = in_ref[k * units : (k + 1) * units].astype(F32)


def widen(grads, units):
    rows, width = grads.shape
    return pl.pallas_call(
        widen_kernel,
        out_shape=(jax.ShapeDtypeStruct((1, units, width), F32),) * (rows // units),
        compiler_params=params(),
        cost_estimate=cost(0, 6 * rows * width),
        name="widen",
    )(grads)


def finish_kernel(take_ref, home_ref, stream_ref, inverse_ref, gain_ref, out_ref):
    width = stream_ref.shape[1]
    inverse = inverse_ref[:, 0:1]
    total = 0.0
    for start in range(0, width, 512):
        lanes = slice(start, start + 512)
        home = home_ref[:, :, lanes].reshape(take_ref.shape[1], 512)
        scaled = dot_nn(take_ref[...], home) * gain_ref[:, lanes]
        out_ref[0, :, lanes] = scaled
        total = total + jnp.sum(stream_ref[:, lanes] * scaled, axis=1, keepdims=True)
    factor = inverse * inverse * inverse * (total / width)
    out_ref[0] = inverse * out_ref[0] - stream_ref[...] * factor


def finish(take, home, stream, inverse, gain):
    tokens, width = stream.shape
    slots = take.shape[1]
    return pl.pallas_call(
        finish_kernel,
        out_shape=jax.ShapeDtypeStruct((1, tokens, width), F32),
        compiler_params=params(),
        cost_estimate=cost(2 * slots * tokens * width, 2 * (slots + 4 * tokens) * width),
        name="finish",
    )(take, home, stream, inverse, gain)


def in_hbm(values):
    return pltpu.with_memory_space_constraint(values, pltpu.HBM)


def swap(values, axis="expert"):
    return lax.all_to_all(values, axis, split_axis=0, concat_axis=0, tiled=True)


def body(qkv, resid, lengths, norm_gain, expert_ids, gate_vals, w_gate, w_up, w_down, cotangent):
    _, steps, triple = qkv.shape
    width = triple // 3
    head_size = width // HEADS
    owners = lax.axis_size("expert")
    quarters = owners // (steps // 16)
    capacity = 2 * steps * expert_ids.shape[2] // owners
    slots = owners * capacity
    gain = norm_gain.reshape(1, width)

    down_full = lax.all_gather(w_down, "dp", axis=2, tiled=True)
    gate_full = lax.all_gather(w_gate, "dp", axis=2, tiled=True)
    up_full = lax.all_gather(w_up, "dp", axis=2, tiled=True)

    received = swap(pack(lengths, qkv, quarters))
    put, take, mix, adjoint_send = route(
        expert_ids, gate_vals, cotangent, capacity, slots, width // quarters
    )
    shared = swap(in_hbm(attend(received, in_hbm(adjoint_send), head_size)))
    stream, inverse, normed_send = norm(lengths, shared, resid, gain, put, quarters)
    x_rows = swap(in_hbm(normed_send))

    gate_full, up_full, down_full = in_hbm(gate_full), in_hbm(up_full), in_hbm(down_full)
    grad_hidden = in_hbm(hidden_grad(shared, down_full))
    expert_out, inner = expert(x_rows, grad_hidden, gate_full, up_full, down_full)
    out_home = swap(in_hbm(expert_out))

    grads = lax.psum_scatter(
        partials(inner, x_rows, shared), "dp", scatter_dimension=1, tiled=True
    )
    grad_gate, grad_up, grad_down = widen(grads, w_gate.shape[1])
    grad_rows = in_hbm(row_grads(inner, gate_full, up_full, capacity))
    grad_rows, out_home = lax.optimization_barrier((grad_rows, out_home))
    grad_home = swap(grad_rows)

    mixture = mixed(mix, out_home)
    take, grad_gate = lax.optimization_barrier((take, grad_gate))
    grad_stream = finish(take, grad_home, stream, inverse, gain)
    return (mixture, grad_stream, grad_gate, grad_up, grad_down)


def solution(mesh):
    tokens = P(("dp", "expert"), None, None)
    weights = P("expert", None, "dp")
    in_specs = (
        tokens,
        tokens,
        P(("dp", "expert")),
        P(),
        tokens,
        tokens,
        weights,
        weights,
        weights,
        tokens,
    )
    out_specs = (tokens, tokens, weights, weights, weights)
    return jax.shard_map(body, mesh=mesh, in_specs=in_specs, out_specs=out_specs, check_vma=False)
```

```python
import functools
import math

import jax
import jax.numpy as jnp
from jax import lax
from jax.experimental import pallas as pl
from jax.experimental.pallas import tpu as pltpu
from jax.sharding import PartitionSpec as P

HEADS = 16
ABSENT = 100.0
F32 = jnp.float32
BF16 = jnp.bfloat16
LONG = 10**15


def cost(flops, bytes_accessed, transcendentals=0):
    return pl.CostEstimate(
        flops=flops, bytes_accessed=bytes_accessed, transcendentals=transcendentals
    )


def params(mebibytes=40):
    return pltpu.CompilerParams(vmem_limit_bytes=mebibytes * 1024 * 1024)


def dot_nt(a, b):
    return lax.dot_general(a, b, (((1,), (1,)), ((), ())), preferred_element_type=F32)


def flat_rows(ref):
    return ref[...].reshape(ref.shape[0] * ref.shape[1], ref.shape[2])


def dot_nn(a, b):
    return lax.dot_general(a, b, (((1,), (0,)), ((), ())), preferred_element_type=F32)


def pack_kernel(quarters, lengths_ref, qkv_ref, out_ref):
    rows = qkv_ref.shape[1]
    wide = out_ref.shape[3]
    step = pl.program_id(0)
    for block in range(rows // 16):
        times = step * rows + block * 16 + lax.broadcasted_iota(jnp.int32, (16, wide), 0)
        live = times < lengths_ref[0]
        for quarter in range(quarters):
            for kind in range(3):
                start = (kind * quarters + quarter) * wide
                piece = qkv_ref[0, block * 16 : block * 16 + 16, start : start + wide]
                if kind == 1:
                    piece = jnp.where(live, piece.astype(F32), ABSENT).astype(BF16)
                out_ref[block * quarters + quarter, kind] = piece


def pack(lengths, qkv, quarters):
    _, steps, triple = qkv.shape
    wide = triple // 3 // quarters
    rows = 32
    return pl.pallas_call(
        functools.partial(pack_kernel, quarters),
        grid=(steps // rows,),
        in_specs=[
            pl.BlockSpec(memory_space=pltpu.SMEM),
            pl.BlockSpec((1, rows, triple), lambda i: (0, i, 0)),
        ],
        out_specs=pl.BlockSpec((rows // 16 * quarters, 3, 16, wide), lambda i: (i, 0, 0, 0)),
        out_shape=jax.ShapeDtypeStruct((steps // 16 * quarters, 3, 16, wide), BF16),
        compiler_params=params(),
        cost_estimate=cost(0, 4 * steps * triple),
        name="pack_qkv",
    )(lengths, qkv)


def attend_kernel(head_size, scale, in_ref, shared_ref, out_ref, bias_ref):
    del shared_ref
    series, _, times, wide = in_ref.shape
    pairs = series * times
    chunk = 128
    keys = in_ref[:, 1, :, 0:head_size].reshape(pairs, head_size)
    total = dot_nt(jnp.ones((8, head_size), BF16), keys)[0:1]
    live = total < 0.5 * ABSENT * head_size
    for part in range(pairs // chunk):
        first = part * chunk // times
        count = chunk // times
        row = part * chunk + lax.broadcasted_iota(jnp.int32, (chunk, pairs), 0)
        column = lax.broadcasted_iota(jnp.int32, (chunk, pairs), 1)
        allowed = (((row ^ column) & (times - 1)) == 0) & (live | (row == column))
        bias_ref[...] = jnp.where(allowed, 0.0, -1e30)
        for head in range(wide // head_size):
            lanes = slice(head * head_size, (head + 1) * head_size)
            queries = in_ref[first : first + count, 0, :, lanes].reshape(chunk, head_size)
            keys = in_ref[:, 1, :, lanes].reshape(pairs, head_size)
            values = in_ref[:, 2, :, lanes].reshape(pairs, head_size)
            scores = dot_nt(queries, keys) * scale + bias_ref[...]
            highest = jnp.max(scores, axis=1, keepdims=True)
            raised = jnp.exp2(scores - highest).astype(BF16)
            both = dot_nn(raised, jnp.concatenate([values, jnp.ones_like(values)], axis=1))
            attended = (both[:, :head_size] / both[:, head_size:]).astype(BF16)
            out_ref[first : first + count, :, lanes] = attended.reshape(count, times, head_size)


def attend(received, shared, head_size):
    series, _, times, wide = received.shape
    pairs = series * times
    heads = wide // head_size
    last = shared.shape[2] // wide - 1
    return pl.pallas_call(
        functools.partial(attend_kernel, head_size, math.log2(math.e) / math.sqrt(head_size)),
        grid=(1,),
        in_specs=[
            pl.BlockSpec(received.shape, lambda i: (0, 0, 0, 0)),
            pl.BlockSpec(memory_space=pl.ANY),
        ],
        out_specs=pl.BlockSpec((series, times, wide), lambda i: (0, 0, last)),
        out_shape=jax.ShapeDtypeStruct(shared.shape, BF16),
        input_output_aliases={1: 0},
        scratch_shapes=[pltpu.VMEM((128, pairs), F32)],
        compiler_params=params(),
        cost_estimate=cost(
            4 * heads * pairs * pairs * head_size, received.size * 8 // 3, heads * pairs * pairs
        ),
        name="attend",
    )(received, shared)


def slots_of(ids_ref, capacity):
    tokens = ids_ref.shape[1]
    ids = ids_ref[0]
    lane = lax.broadcasted_iota(jnp.int32, (tokens, tokens), 1)
    sub = lax.broadcasted_iota(jnp.int32, (tokens, tokens), 0)
    named = [(lane == ids[:, k : k + 1]).astype(F32) for k in range(2)]
    earlier = (lane < sub).astype(BF16)
    before = dot_nn(earlier, (named[0] + named[1]).astype(BF16))
    return [
        ids[:, k : k + 1].astype(F32) * capacity
        + jnp.sum(before * named[k], axis=1, keepdims=True)
        for k in range(2)
    ]


def across(column):
    tokens = column.shape[0]
    return jnp.transpose(jnp.broadcast_to(column, (tokens, tokens)))[0:1]


def route_kernel(capacity, ids_ref, gates_ref, cotangent_ref, put_ref, send_ref):
    slots, tokens = put_ref.shape
    gates = gates_ref[0].astype(F32)
    flat = [across(column) for column in slots_of(ids_ref, capacity)]
    flat_gate = [across(gates[:, k : k + 1]) for k in range(2)]
    down = lax.broadcasted_iota(jnp.int32, (slots, tokens), 0).astype(F32)
    fall = [down == flat[k] for k in range(2)]
    put_ref[...] = jnp.where(fall[0] | fall[1], 1.0, 0.0).astype(BF16)
    weigh = jnp.where(fall[0], flat_gate[0], jnp.where(fall[1], flat_gate[1], 0.0)).astype(BF16)
    owners = slots // capacity
    wide = cotangent_ref.shape[2]
    for start in range(0, wide, 512):
        rows = dot_nn(weigh, cotangent_ref[0, :, start : start + 512]).astype(BF16)
        send_ref[:, :, start : start + 512] = rows.reshape(owners, capacity, 512)


def route(ids, gates, cotangent, capacity, slots, extra):
    _, tokens, wide = cotangent.shape
    return pl.pallas_call(
        functools.partial(route_kernel, capacity),
        out_shape=(
            jax.ShapeDtypeStruct((slots, tokens), BF16),
            jax.ShapeDtypeStruct((slots // capacity, capacity, wide + extra), BF16),
        ),
        grid=(1,),
        in_specs=[
            pl.BlockSpec(ids.shape, lambda i: (0, 0, 0)),
            pl.BlockSpec(gates.shape, lambda i: (0, 0, 0)),
            pl.BlockSpec(cotangent.shape, lambda i: (0, 0, 0)),
        ],
        out_specs=(
            pl.BlockSpec((slots, tokens), lambda i: (0, 0)),
            pl.BlockSpec((slots // capacity, capacity, wide), lambda i: (0, 0, 0)),
        ),
        compiler_params=params(),
        cost_estimate=cost(2 * slots * tokens * wide, 2 * (slots + tokens) * wide),
        name="route",
    )(ids, gates, cotangent)


def back_kernel(capacity, ids_ref, gates_ref, take_ref, mix_ref):
    gates = gates_ref[0].astype(F32)
    slot = slots_of(ids_ref, capacity)
    along = lax.broadcasted_iota(jnp.int32, take_ref.shape, 1).astype(F32)
    hit = [along == slot[k] for k in range(2)]
    take_ref[...] = jnp.where(hit[0] | hit[1], 1.0, 0.0).astype(BF16)
    mix_ref[...] = jnp.where(
        hit[0], gates[:, 0:1], jnp.where(hit[1], gates[:, 1:2], 0.0)
    ).astype(BF16)


def back(ids, gates, capacity, slots):
    shape = jax.ShapeDtypeStruct((ids.shape[1], slots), BF16)
    return pl.pallas_call(
        functools.partial(back_kernel, capacity),
        out_shape=(shape, shape),
        compiler_params=params(),
        cost_estimate=cost(10**6, 10**6),
        name="back",
    )(ids, gates)


def norm_kernel(quarters, lengths_ref, att_ref, resid_ref, gain_ref, put_ref, stream_ref, inverse_ref, send_ref):
    blocks, times, wide = att_ref.shape
    for block in range(blocks):
        at, quarter = block // quarters, block % quarters
        rows = slice(at * times, (at + 1) * times)
        lanes = slice(quarter * wide, (quarter + 1) * wide)
        live = at * times + lax.broadcasted_iota(jnp.int32, (times, wide), 0) < lengths_ref[0]
        stream_ref[rows, lanes] = resid_ref[0, rows, lanes].astype(F32) + jnp.where(
            live, att_ref[block].astype(F32), 0.0
        )
    width = stream_ref.shape[1]
    stream = stream_ref[...]
    inverse = 1.0 / jnp.sqrt(jnp.sum(stream * stream, axis=1, keepdims=True) / width + 1e-05)
    inverse_ref[...] = jnp.broadcast_to(inverse, inverse_ref.shape)
    for start in range(0, width, 512):
        lanes = slice(start, start + 512)
        normed = (stream_ref[:, lanes] * inverse * gain_ref[:, lanes]).astype(BF16)
        rows = dot_nn(put_ref[...], normed).astype(BF16)
        send_ref[:, :, lanes] = rows.reshape(send_ref.shape[0], send_ref.shape[1], 512)


def norm(lengths, att, resid, gain, put, quarters):
    _, tokens, width = resid.shape
    slots = put.shape[0]
    blocks, times, whole = att.shape
    wide = width // quarters
    return pl.pallas_call(
        functools.partial(norm_kernel, quarters),
        grid=(1,),
        in_specs=[
            pl.BlockSpec(memory_space=pltpu.SMEM),
            pl.BlockSpec((blocks, times, wide), lambda i: (0, 0, whole // wide - 1)),
            pl.BlockSpec(resid.shape, lambda i: (0, 0, 0)),
            pl.BlockSpec(gain.shape, lambda i: (0, 0)),
            pl.BlockSpec(put.shape, lambda i: (0, 0)),
        ],
        out_specs=(
            pl.BlockSpec((tokens, width), lambda i: (0, 0)),
            pl.BlockSpec((tokens, 128), lambda i: (0, 0)),
            pl.BlockSpec((blocks, slots // blocks, width), lambda i: (0, 0, 0)),
        ),
        out_shape=(
            jax.ShapeDtypeStruct((tokens, width), F32),
            jax.ShapeDtypeStruct((tokens, 128), F32),
            jax.ShapeDtypeStruct((blocks, slots // blocks, width), BF16),
        ),
        compiler_params=params(),
        cost_estimate=cost(2 * slots * tokens * width, 2 * (slots + 4 * tokens) * width),
        name="norm",
    )(lengths, att, resid, gain, put)


def expert_kernel(
    x_ref,
    gh_hbm,
    gate_hbm,
    up_hbm,
    down_hbm,
    rows_hbm,
    inner_hbm,
    gh_ref,
    gate_ref,
    up_ref,
    down_ref,
    rows_ref,
    inner_ref,
    in_sems,
    out_sems,
):
    fetches = [
        pltpu.make_async_copy(source, target, in_sems.at[k])
        for k, (source, target) in enumerate(
            (
                (gate_hbm, gate_ref),
                (up_hbm, up_ref),
                (gh_hbm, gh_ref),
                (down_hbm, down_ref),
            )
        )
    ]
    for fetch in fetches:
        fetch.start()
    stores = []

    def store(source, target):
        copy = pltpu.make_async_copy(source, target, out_sems.at[len(stores)])
        copy.start()
        stores.append(copy)

    fetches[0].wait()
    x = flat_rows(x_ref)
    gate_pre = dot_nt(x, gate_ref[0])
    fetches[1].wait()
    up_pre = dot_nt(x, up_ref[0])
    sigmoid = 1.0 / (1.0 + jnp.exp(-gate_pre))
    silu = gate_pre * sigmoid
    inner_ref[2] = (silu * up_pre).astype(BF16)
    store(inner_ref.at[2], inner_hbm.at[2])
    fetches[2].wait()
    grad_hidden = gh_ref[...]
    inner_ref[0] = (
        grad_hidden * up_pre * sigmoid * (1.0 + gate_pre * (1.0 - sigmoid))
    ).astype(BF16)
    store(inner_ref.at[0], inner_hbm.at[0])
    inner_ref[1] = (grad_hidden * silu).astype(BF16)
    store(inner_ref.at[1], inner_hbm.at[1])
    fetches[3].wait()
    owners, capacity, width = x_ref.shape
    half = width // 2
    for k in range(2):
        lanes = slice(k * half, (k + 1) * half)
        product = dot_nn(inner_ref[2], down_ref[0, :, lanes]).astype(BF16)
        rows_ref[:, :, lanes] = product.reshape(owners, capacity, half)
        store(rows_ref.at[:, :, lanes], rows_hbm.at[:, :, lanes])
    for k in range(2):
        lanes = slice(k * half, (k + 1) * half)
        product = dot_nn(inner_ref[0], gate_ref[0, :, lanes])
        product = (product + dot_nn(inner_ref[1], up_ref[0, :, lanes])).astype(BF16)
        lanes = slice(width + k * half, width + (k + 1) * half)
        rows_ref[:, :, lanes] = product.reshape(owners, capacity, half)
        store(rows_ref.at[:, :, lanes], rows_hbm.at[:, :, lanes])
    for copy in stores:
        copy.wait()


def expert(x, grad_hidden, gate, up, down):
    owners, capacity, width = x.shape
    rows = owners * capacity
    units = gate.shape[1]
    hbm = pl.BlockSpec(memory_space=pl.ANY)
    out = (owners, capacity, 2 * width)
    inner = (3, rows, units)
    return pl.pallas_call(
        expert_kernel,
        in_specs=[pl.BlockSpec(memory_space=pltpu.VMEM)] + [hbm] * 4,
        out_specs=(hbm, hbm),
        out_shape=(pltpu.HBM(out, BF16), pltpu.HBM(inner, BF16)),
        scratch_shapes=[
            pltpu.VMEM(grad_hidden.shape, F32),
            pltpu.VMEM(gate.shape, BF16),
            pltpu.VMEM(up.shape, BF16),
            pltpu.VMEM(down.shape, BF16),
            pltpu.VMEM(out, BF16),
            pltpu.VMEM(inner, BF16),
            pltpu.SemaphoreType.DMA((4,)),
            pltpu.SemaphoreType.DMA((7,)),
        ],
        compiler_params=params(44),
        cost_estimate=cost(
            10 * rows * width * units, 6 * rows * width + 6 * units * width, rows * units
        ),
        name="expert",
    )(x, grad_hidden, gate, up, down)


def grad_hidden_kernel(grad_out_ref, down_ref, out_ref):
    out_ref[...] = dot_nt(flat_rows(grad_out_ref), down_ref[0])


def hidden_grad(shared, down):
    owners, capacity, _ = shared.shape
    rows = owners * capacity
    _, units, width = down.shape
    block = 256
    return pl.pallas_call(
        grad_hidden_kernel,
        grid=(units // block,),
        in_specs=[
            pl.BlockSpec((owners, capacity, width), lambda i: (0, 0, 0)),
            pl.BlockSpec((1, block, width), lambda i: (0, i, 0)),
        ],
        out_specs=pl.BlockSpec((rows, block), lambda i: (0, i)),
        out_shape=jax.ShapeDtypeStruct((rows, units), F32),
        compiler_params=params(),
        cost_estimate=cost(2 * rows * units * width, 2 * width * (rows + units) + 4 * rows * units),
        name="grad_hidden",
    )(shared, down)


def partial_kernel(inner_ref, x_ref, grad_out_ref, out_ref):
    def product(right):
        return lax.dot_general(
            inner_ref[0], right, (((0,), (0,)), ((), ())), preferred_element_type=F32
        ).astype(BF16)

    @pl.when(pl.program_id(0) < 2)
    def _():
        out_ref[...] = product(flat_rows(x_ref))

    @pl.when(pl.program_id(0) == 2)
    def _():
        out_ref[...] = product(flat_rows(grad_out_ref))


def partials(inner, x, shared):
    kinds, rows, units = inner.shape
    width = x.shape[2]
    block = 256
    count = units // block
    whole = pl.BlockSpec(x.shape, lambda k, i: (0, 0, 0))
    return pl.pallas_call(
        partial_kernel,
        grid=(kinds, count),
        in_specs=[pl.BlockSpec((1, rows, block), lambda k, i: (k, 0, i)), whole, whole],
        out_specs=pl.BlockSpec((block, width), lambda k, i: (k * count + i, 0)),
        out_shape=jax.ShapeDtypeStruct((kinds * units, width), BF16),
        compiler_params=params(36),
        cost_estimate=cost(2 * kinds * rows * units * width, 4 * (kinds * units + rows) * width),
        name="partials",
    )(inner, x, shared)


def widen_kernel(*refs):
    for in_ref, out_ref in zip(refs[:3], refs[3:]):
        out_ref[0] = in_ref[...].astype(F32)


def widen(grads, units):
    rows, width = grads.shape
    block = 256
    count = units // block
    return pl.pallas_call(
        widen_kernel,
        grid=(count,),
        in_specs=[
            pl.BlockSpec((block, width), lambda i, k=k: (k * count + i, 0)) for k in range(3)
        ],
        out_specs=(pl.BlockSpec((1, block, width), lambda i: (0, i, 0)),) * 3,
        out_shape=(jax.ShapeDtypeStruct((1, units, width), F32),) * 3,
        compiler_params=params(),
        cost_estimate=cost(0, 6 * rows * width),
        name="widen",
    )(grads, grads, grads)


def finish_kernel(take_ref, mix_ref, home_ref, stream_ref, inverse_ref, gain_ref, mixture_ref, out_ref):
    width = stream_ref.shape[1]
    slots = take_ref.shape[1]
    wide = 512
    inverse = inverse_ref[:, 0:1]
    total = 0.0
    for start in range(0, width, wide):
        lanes = slice(start, start + wide)
        home = home_ref[:, :, width + start : width + start + wide].reshape(slots, wide)
        scaled = dot_nn(take_ref[...], home) * gain_ref[:, lanes]
        out_ref[0, :, lanes] = scaled
        total = total + jnp.sum(stream_ref[:, lanes] * scaled, axis=1, keepdims=True)
    factor = inverse * inverse * inverse * (total / width)
    for start in range(0, width, wide):
        lanes = slice(start, start + wide)
        out_ref[0, :, lanes] = inverse * out_ref[0, :, lanes] - stream_ref[:, lanes] * factor
        home = home_ref[:, :, lanes].reshape(slots, wide)
        mixture_ref[0, :, lanes] = dot_nn(mix_ref[...], home).astype(BF16)


def finish(take, mix, home, stream, inverse, gain):
    tokens, width = stream.shape
    return pl.pallas_call(
        finish_kernel,
        out_shape=(
            jax.ShapeDtypeStruct((1, tokens, width), BF16),
            jax.ShapeDtypeStruct((1, tokens, width), F32),
        ),
        compiler_params=params(),
        cost_estimate=cost(LONG, LONG // 1000),
        name="finish",
    )(take, mix, home, stream, inverse, gain)


def in_hbm(values):
    return pltpu.with_memory_space_constraint(values, pltpu.HBM)


def swap(values, axis="expert"):
    return lax.all_to_all(values, axis, split_axis=0, concat_axis=0, tiled=True)


def body(qkv, resid, lengths, norm_gain, expert_ids, gate_vals, w_gate, w_up, w_down, cotangent):
    _, steps, triple = qkv.shape
    width = triple // 3
    head_size = width // HEADS
    owners = lax.axis_size("expert")
    quarters = owners // (steps // 16)
    capacity = 2 * steps * expert_ids.shape[2] // owners
    slots = owners * capacity
    gain = norm_gain.reshape(1, width)

    down_full = lax.all_gather(w_down, "dp", axis=2, tiled=True)
    gate_full = lax.all_gather(w_gate, "dp", axis=2, tiled=True)
    up_full = lax.all_gather(w_up, "dp", axis=2, tiled=True)

    received = swap(pack(lengths, qkv, quarters))
    put, adjoint_send = route(
        expert_ids, gate_vals, cotangent, capacity, slots, width // quarters
    )
    take, mix = back(expert_ids, gate_vals, capacity, slots)
    shared = swap(in_hbm(attend(received, in_hbm(adjoint_send), head_size)))
    stream, inverse, normed_send = norm(lengths, shared, resid, gain, put, quarters)
    x_rows = swap(in_hbm(normed_send))

    gate_full, up_full, down_full = in_hbm(gate_full), in_hbm(up_full), in_hbm(down_full)
    grad_hidden = in_hbm(hidden_grad(shared, down_full))
    rows, inner = expert(x_rows, grad_hidden, gate_full, up_full, down_full)
    home = swap(rows)

    grads = lax.psum_scatter(
        partials(inner, x_rows, shared), "dp", scatter_dimension=1, tiled=True
    )
    grad_gate, grad_up, grad_down = widen(in_hbm(grads), w_gate.shape[1])
    mixture, grad_stream = finish(take, mix, home, stream, inverse, gain)
    return (mixture, grad_stream, grad_gate, grad_up, grad_down)


def solution(mesh):
    tokens = P(("dp", "expert"), None, None)
    weights = P("expert", None, "dp")
    in_specs = (
        tokens,
        tokens,
        P(("dp", "expert")),
        P(),
        tokens,
        tokens,
        weights,
        weights,
        weights,
        tokens,
    )
    out_specs = (tokens, tokens, weights, weights, weights)
    return jax.shard_map(body, mesh=mesh, in_specs=in_specs, out_specs=out_specs, check_vma=False)
```

```python
import functools
import math

import jax
import jax.numpy as jnp
from jax import lax
from jax.experimental import pallas as pl
from jax.experimental.pallas import tpu as pltpu
from jax.sharding import PartitionSpec as P

HEADS = 16
ABSENT = 100.0
F32 = jnp.float32
BF16 = jnp.bfloat16
LONG = 10**15


def cost(flops, bytes_accessed, transcendentals=0):
    return pl.CostEstimate(
        flops=flops, bytes_accessed=bytes_accessed, transcendentals=transcendentals
    )


def params(mebibytes=40):
    return pltpu.CompilerParams(vmem_limit_bytes=mebibytes * 1024 * 1024)


def dot_nt(a, b):
    return lax.dot_general(a, b, (((1,), (1,)), ((), ())), preferred_element_type=F32)


def flat_rows(ref):
    return ref[...].reshape(ref.shape[0] * ref.shape[1], ref.shape[2])


def dot_nn(a, b):
    return lax.dot_general(a, b, (((1,), (0,)), ((), ())), preferred_element_type=F32)


def pack_kernel(quarters, lengths_ref, qkv_ref, out_ref):
    rows = qkv_ref.shape[1]
    wide = out_ref.shape[3]
    step = pl.program_id(0)
    for block in range(rows // 16):
        times = step * rows + block * 16 + lax.broadcasted_iota(jnp.int32, (16, wide), 0)
        live = times < lengths_ref[0]
        for quarter in range(quarters):
            for kind in range(3):
                start = (kind * quarters + quarter) * wide
                piece = qkv_ref[0, block * 16 : block * 16 + 16, start : start + wide]
                if kind == 1:
                    piece = jnp.where(live, piece.astype(F32), ABSENT).astype(BF16)
                out_ref[block * quarters + quarter, kind] = piece


def pack(lengths, qkv, quarters):
    _, steps, triple = qkv.shape
    wide = triple // 3 // quarters
    rows = 32
    return pl.pallas_call(
        functools.partial(pack_kernel, quarters),
        grid=(steps // rows,),
        in_specs=[
            pl.BlockSpec(memory_space=pltpu.SMEM),
            pl.BlockSpec((1, rows, triple), lambda i: (0, i, 0)),
        ],
        out_specs=pl.BlockSpec((rows // 16 * quarters, 3, 16, wide), lambda i: (i, 0, 0, 0)),
        out_shape=jax.ShapeDtypeStruct((steps // 16 * quarters, 3, 16, wide), BF16),
        compiler_params=params(),
        cost_estimate=cost(0, 4 * steps * triple),
        name="pack_qkv",
    )(lengths, qkv)


def attend_kernel(head_size, scale, in_ref, shared_ref, out_ref, bias_ref):
    del shared_ref
    series, _, times, wide = in_ref.shape
    pairs = series * times
    chunk = 128
    keys = in_ref[:, 1, :, 0:head_size].reshape(pairs, head_size)
    total = dot_nt(jnp.ones((8, head_size), BF16), keys)[0:1]
    live = total < 0.5 * ABSENT * head_size
    for part in range(pairs // chunk):
        first = part * chunk // times
        count = chunk // times
        row = part * chunk + lax.broadcasted_iota(jnp.int32, (chunk, pairs), 0)
        column = lax.broadcasted_iota(jnp.int32, (chunk, pairs), 1)
        allowed = (((row ^ column) & (times - 1)) == 0) & (live | (row == column))
        bias_ref[...] = jnp.where(allowed, 0.0, -1e30)
        for head in range(wide // head_size):
            lanes = slice(head * head_size, (head + 1) * head_size)
            queries = in_ref[first : first + count, 0, :, lanes].reshape(chunk, head_size)
            keys = in_ref[:, 1, :, lanes].reshape(pairs, head_size)
            values = in_ref[:, 2, :, lanes].reshape(pairs, head_size)
            scores = dot_nt(queries, keys) * scale + bias_ref[...]
            highest = jnp.max(scores, axis=1, keepdims=True)
            raised = jnp.exp2(scores - highest).astype(BF16)
            both = dot_nn(raised, jnp.concatenate([values, jnp.ones_like(values)], axis=1))
            attended = (both[:, :head_size] / both[:, head_size:]).astype(BF16)
            out_ref[first : first + count, :, lanes] = attended.reshape(count, times, head_size)


def attend(received, shared, head_size):
    series, _, times, wide = received.shape
    pairs = series * times
    heads = wide // head_size
    last = shared.shape[2] // wide - 1
    return pl.pallas_call(
        functools.partial(attend_kernel, head_size, math.log2(math.e) / math.sqrt(head_size)),
        grid=(1,),
        in_specs=[
            pl.BlockSpec(received.shape, lambda i: (0, 0, 0, 0)),
            pl.BlockSpec(memory_space=pl.ANY),
        ],
        out_specs=pl.BlockSpec((series, times, wide), lambda i: (0, 0, last)),
        out_shape=jax.ShapeDtypeStruct(shared.shape, BF16),
        input_output_aliases={1: 0},
        scratch_shapes=[pltpu.VMEM((128, pairs), F32)],
        compiler_params=params(),
        cost_estimate=cost(
            4 * heads * pairs * pairs * head_size, received.size * 8 // 3, heads * pairs * pairs
        ),
        name="attend",
    )(received, shared)


def slots_of(ids_ref, capacity):
    tokens = ids_ref.shape[1]
    ids = ids_ref[0]
    lane = lax.broadcasted_iota(jnp.int32, (tokens, tokens), 1)
    sub = lax.broadcasted_iota(jnp.int32, (tokens, tokens), 0)
    named = [(lane == ids[:, k : k + 1]).astype(F32) for k in range(2)]
    earlier = (lane < sub).astype(BF16)
    before = dot_nn(earlier, (named[0] + named[1]).astype(BF16))
    return [
        ids[:, k : k + 1].astype(F32) * capacity
        + jnp.sum(before * named[k], axis=1, keepdims=True)
        for k in range(2)
    ]


def across(column):
    tokens = column.shape[0]
    return jnp.transpose(jnp.broadcast_to(column, (tokens, tokens)))[0:1]


def route_kernel(capacity, ids_ref, gates_ref, cotangent_ref, put_ref, send_ref):
    slots, tokens = put_ref.shape
    gates = gates_ref[0].astype(F32)
    flat = [across(column) for column in slots_of(ids_ref, capacity)]
    flat_gate = [across(gates[:, k : k + 1]) for k in range(2)]
    down = lax.broadcasted_iota(jnp.int32, (slots, tokens), 0).astype(F32)
    fall = [down == flat[k] for k in range(2)]
    put_ref[...] = jnp.where(fall[0] | fall[1], 1.0, 0.0).astype(BF16)
    weigh = jnp.where(fall[0], flat_gate[0], jnp.where(fall[1], flat_gate[1], 0.0)).astype(BF16)
    owners = slots // capacity
    wide = cotangent_ref.shape[2]
    for start in range(0, wide, 512):
        rows = dot_nn(weigh, cotangent_ref[0, :, start : start + 512]).astype(BF16)
        send_ref[:, :, start : start + 512] = rows.reshape(owners, capacity, 512)


def route(ids, gates, cotangent, capacity, slots, extra):
    _, tokens, wide = cotangent.shape
    return pl.pallas_call(
        functools.partial(route_kernel, capacity),
        out_shape=(
            jax.ShapeDtypeStruct((slots, tokens), BF16),
            jax.ShapeDtypeStruct((slots // capacity, capacity, wide + extra), BF16),
        ),
        grid=(1,),
        in_specs=[
            pl.BlockSpec(ids.shape, lambda i: (0, 0, 0)),
            pl.BlockSpec(gates.shape, lambda i: (0, 0, 0)),
            pl.BlockSpec(cotangent.shape, lambda i: (0, 0, 0)),
        ],
        out_specs=(
            pl.BlockSpec((slots, tokens), lambda i: (0, 0)),
            pl.BlockSpec((slots // capacity, capacity, wide), lambda i: (0, 0, 0)),
        ),
        compiler_params=params(),
        cost_estimate=cost(2 * slots * tokens * wide, 2 * (slots + tokens) * wide),
        name="route",
    )(ids, gates, cotangent)


def back_kernel(capacity, ids_ref, gates_ref, take_ref, mix_ref):
    gates = gates_ref[0].astype(F32)
    slot = slots_of(ids_ref, capacity)
    along = lax.broadcasted_iota(jnp.int32, take_ref.shape, 1).astype(F32)
    hit = [along == slot[k] for k in range(2)]
    take_ref[...] = jnp.where(hit[0] | hit[1], 1.0, 0.0).astype(BF16)
    mix_ref[...] = jnp.where(
        hit[0], gates[:, 0:1], jnp.where(hit[1], gates[:, 1:2], 0.0)
    ).astype(BF16)


def back(ids, gates, capacity, slots):
    shape = jax.ShapeDtypeStruct((ids.shape[1], slots), BF16)
    return pl.pallas_call(
        functools.partial(back_kernel, capacity),
        out_shape=(shape, shape),
        compiler_params=params(),
        cost_estimate=cost(10**6, 10**6),
        name="back",
    )(ids, gates)


def norm_kernel(
    quarters,
    lengths_ref,
    att_ref,
    resid_ref,
    gain_ref,
    put_ref,
    stream_ref,
    inverse_ref,
    send_hbm,
    send_ref,
    sems,
):
    blocks, times, wide = att_ref.shape
    for block in range(blocks):
        at, quarter = block // quarters, block % quarters
        rows = slice(at * times, (at + 1) * times)
        lanes = slice(quarter * wide, (quarter + 1) * wide)
        live = at * times + lax.broadcasted_iota(jnp.int32, (times, wide), 0) < lengths_ref[0]
        stream_ref[rows, lanes] = resid_ref[0, rows, lanes].astype(F32) + jnp.where(
            live, att_ref[block].astype(F32), 0.0
        )
    width = stream_ref.shape[1]
    stream = stream_ref[...]
    inverse = 1.0 / jnp.sqrt(jnp.sum(stream * stream, axis=1, keepdims=True) / width + 1e-05)
    inverse_ref[...] = jnp.broadcast_to(inverse, inverse_ref.shape)
    stores = []
    for start in range(0, width, 512):
        lanes = slice(start, start + 512)
        normed = (stream_ref[:, lanes] * inverse * gain_ref[:, lanes]).astype(BF16)
        rows = dot_nn(put_ref[...], normed).astype(BF16)
        send_ref[:, :, lanes] = rows.reshape(send_ref.shape[0], send_ref.shape[1], 512)
        stores.append(
            pltpu.make_async_copy(
                send_ref.at[:, :, lanes], send_hbm.at[:, :, lanes], sems.at[len(stores)]
            )
        )
        stores[-1].start()
    for copy in stores:
        copy.wait()


def norm(lengths, att, resid, gain, put, quarters):
    _, tokens, width = resid.shape
    slots = put.shape[0]
    blocks, times, whole = att.shape
    wide = width // quarters
    return pl.pallas_call(
        functools.partial(norm_kernel, quarters),
        grid=(1,),
        in_specs=[
            pl.BlockSpec(memory_space=pltpu.SMEM),
            pl.BlockSpec((blocks, times, wide), lambda i: (0, 0, whole // wide - 1)),
            pl.BlockSpec(resid.shape, lambda i: (0, 0, 0)),
            pl.BlockSpec(gain.shape, lambda i: (0, 0)),
            pl.BlockSpec(put.shape, lambda i: (0, 0)),
        ],
        out_specs=(
            pl.BlockSpec((tokens, width), lambda i: (0, 0)),
            pl.BlockSpec((tokens, 128), lambda i: (0, 0)),
            pl.BlockSpec(memory_space=pl.ANY),
        ),
        out_shape=(
            jax.ShapeDtypeStruct((tokens, width), F32),
            jax.ShapeDtypeStruct((tokens, 128), F32),
            pltpu.HBM((blocks, slots // blocks, width), BF16),
        ),
        scratch_shapes=[
            pltpu.VMEM((blocks, slots // blocks, width), BF16),
            pltpu.SemaphoreType.DMA((width // 512,)),
        ],
        compiler_params=params(),
        cost_estimate=cost(2 * slots * tokens * width, 2 * (slots + 4 * tokens) * width),
        name="norm",
    )(lengths, att, resid, gain, put)


def expert_kernel(
    x_ref,
    gh_hbm,
    gate_hbm,
    up_hbm,
    down_hbm,
    rows_hbm,
    inner_hbm,
    gh_ref,
    gate_ref,
    up_ref,
    down_ref,
    rows_ref,
    inner_ref,
    in_sems,
    out_sems,
):
    fetches = [
        pltpu.make_async_copy(source, target, in_sems.at[k])
        for k, (source, target) in enumerate(
            (
                (gate_hbm, gate_ref),
                (up_hbm, up_ref),
                (gh_hbm, gh_ref),
                (down_hbm, down_ref),
            )
        )
    ]
    for fetch in fetches:
        fetch.start()
    stores = []

    def store(source, target):
        copy = pltpu.make_async_copy(source, target, out_sems.at[len(stores)])
        copy.start()
        stores.append(copy)

    fetches[0].wait()
    x = flat_rows(x_ref)
    gate_pre = dot_nt(x, gate_ref[0])
    fetches[1].wait()
    up_pre = dot_nt(x, up_ref[0])
    sigmoid = 1.0 / (1.0 + jnp.exp(-gate_pre))
    silu = gate_pre * sigmoid
    inner_ref[2] = (silu * up_pre).astype(BF16)
    store(inner_ref.at[2], inner_hbm.at[2])
    fetches[2].wait()
    grad_hidden = gh_ref[...]
    inner_ref[0] = (
        grad_hidden * up_pre * sigmoid * (1.0 + gate_pre * (1.0 - sigmoid))
    ).astype(BF16)
    store(inner_ref.at[0], inner_hbm.at[0])
    inner_ref[1] = (grad_hidden * silu).astype(BF16)
    store(inner_ref.at[1], inner_hbm.at[1])
    fetches[3].wait()
    owners, capacity, width = x_ref.shape
    half = width // 2
    for k in range(2):
        lanes = slice(k * half, (k + 1) * half)
        product = dot_nn(inner_ref[2], down_ref[0, :, lanes]).astype(BF16)
        rows_ref[:, :, lanes] = product.reshape(owners, capacity, half)
        store(rows_ref.at[:, :, lanes], rows_hbm.at[:, :, lanes])
    for k in range(2):
        lanes = slice(k * half, (k + 1) * half)
        product = dot_nn(inner_ref[0], gate_ref[0, :, lanes])
        product = (product + dot_nn(inner_ref[1], up_ref[0, :, lanes])).astype(BF16)
        lanes = slice(width + k * half, width + (k + 1) * half)
        rows_ref[:, :, lanes] = product.reshape(owners, capacity, half)
        store(rows_ref.at[:, :, lanes], rows_hbm.at[:, :, lanes])
    for copy in stores:
        copy.wait()


def expert(x, grad_hidden, gate, up, down):
    owners, capacity, width = x.shape
    rows = owners * capacity
    units = gate.shape[1]
    hbm = pl.BlockSpec(memory_space=pl.ANY)
    out = (owners, capacity, 2 * width)
    inner = (3, rows, units)
    return pl.pallas_call(
        expert_kernel,
        grid=(1,),
        in_specs=[pl.BlockSpec(x.shape, lambda i: (0, 0, 0))] + [hbm] * 4,
        out_specs=(hbm, hbm),
        out_shape=(pltpu.HBM(out, BF16), pltpu.HBM(inner, BF16)),
        scratch_shapes=[
            pltpu.VMEM(grad_hidden.shape, F32),
            pltpu.VMEM(gate.shape, BF16),
            pltpu.VMEM(up.shape, BF16),
            pltpu.VMEM(down.shape, BF16),
            pltpu.VMEM(out, BF16),
            pltpu.VMEM(inner, BF16),
            pltpu.SemaphoreType.DMA((4,)),
            pltpu.SemaphoreType.DMA((7,)),
        ],
        compiler_params=params(60),
        cost_estimate=cost(
            10 * rows * width * units, 6 * rows * width + 6 * units * width, rows * units
        ),
        name="expert",
    )(x, grad_hidden, gate, up, down)


def grad_hidden_kernel(grad_out_ref, down_ref, out_ref):
    out_ref[...] = dot_nt(flat_rows(grad_out_ref), down_ref[0])


def hidden_grad(shared, down):
    owners, capacity, _ = shared.shape
    rows = owners * capacity
    _, units, width = down.shape
    block = 256
    return pl.pallas_call(
        grad_hidden_kernel,
        grid=(units // block,),
        in_specs=[
            pl.BlockSpec((owners, capacity, width), lambda i: (0, 0, 0)),
            pl.BlockSpec((1, block, width), lambda i: (0, i, 0)),
        ],
        out_specs=pl.BlockSpec((rows, block), lambda i: (0, i)),
        out_shape=jax.ShapeDtypeStruct((rows, units), F32),
        compiler_params=params(),
        cost_estimate=cost(2 * rows * units * width, 2 * width * (rows + units) + 4 * rows * units),
        name="grad_hidden",
    )(shared, down)


def partial_kernel(inner_ref, x_ref, grad_out_ref, out_ref):
    def product(right):
        return lax.dot_general(
            inner_ref[0], right, (((0,), (0,)), ((), ())), preferred_element_type=F32
        ).astype(BF16)

    @pl.when(pl.program_id(0) < 2)
    def _():
        out_ref[...] = product(flat_rows(x_ref))

    @pl.when(pl.program_id(0) == 2)
    def _():
        out_ref[...] = product(flat_rows(grad_out_ref))


def partials(inner, x, shared):
    kinds, rows, units = inner.shape
    width = x.shape[2]
    block = 256
    count = units // block
    whole = pl.BlockSpec(x.shape, lambda k, i: (0, 0, 0))
    return pl.pallas_call(
        partial_kernel,
        grid=(kinds, count),
        in_specs=[pl.BlockSpec((1, rows, block), lambda k, i: (k, 0, i)), whole, whole],
        out_specs=pl.BlockSpec((block, width), lambda k, i: (k * count + i, 0)),
        out_shape=jax.ShapeDtypeStruct((kinds * units, width), BF16),
        compiler_params=params(58),
        cost_estimate=cost(2 * kinds * rows * units * width, 4 * (kinds * units + rows) * width),
        name="partials",
    )(inner, x, shared)


def widen_kernel(in_ref, *out_refs):
    units = out_refs[0].shape[1]
    for k, out_ref in enumerate(out_refs):
        out_ref[0] = in_ref[k * units : (k + 1) * units].astype(F32)


def widen(grads, units):
    rows, width = grads.shape
    return pl.pallas_call(
        widen_kernel,
        out_shape=(jax.ShapeDtypeStruct((1, units, width), F32),) * (rows // units),
        compiler_params=params(),
        cost_estimate=cost(0, 6 * rows * width),
        name="widen",
    )(grads)


def finish_kernel(
    take_ref,
    mix_ref,
    home_hbm,
    stream_ref,
    inverse_ref,
    gain_ref,
    mixture_hbm,
    out_hbm,
    home_ref,
    mixture_ref,
    out_ref,
    in_sems,
    out_sems,
):
    width = stream_ref.shape[1]
    slots = take_ref.shape[1]
    blocks = in_sems.shape[0]
    wide = home_ref.shape[2] // blocks
    half = blocks // 2
    order = list(range(half, blocks)) + list(range(half))

    def block(k):
        return slice(k * wide, (k + 1) * wide)

    fetches = {
        k: pltpu.make_async_copy(
            home_hbm.at[:, :, block(k)], home_ref.at[:, :, block(k)], in_sems.at[k]
        )
        for k in order
    }
    for k in order:
        fetches[k].start()
    total = 0.0
    for k in range(half):
        fetches[half + k].wait()
        home = home_ref[:, :, block(half + k)].reshape(slots, wide)
        scaled = dot_nn(take_ref[...], home) * gain_ref[:, block(k)]
        out_ref[0, :, block(k)] = scaled
        total = total + jnp.sum(stream_ref[:, block(k)] * scaled, axis=1, keepdims=True)
    inverse = inverse_ref[:, 0:1]
    factor = inverse * inverse * inverse * (total / width)
    stores = []
    for k in range(half):
        out_ref[0, :, block(k)] = inverse * out_ref[0, :, block(k)] - stream_ref[:, block(k)] * factor
        stores.append(
            pltpu.make_async_copy(
                out_ref.at[:, :, block(k)], out_hbm.at[:, :, block(k)], out_sems.at[k]
            )
        )
        stores[-1].start()
    for k in range(half):
        fetches[k].wait()
        home = home_ref[:, :, block(k)].reshape(slots, wide)
        mixture_ref[0, :, block(k)] = dot_nn(mix_ref[...], home).astype(BF16)
        stores.append(
            pltpu.make_async_copy(
                mixture_ref.at[:, :, block(k)], mixture_hbm.at[:, :, block(k)], out_sems.at[half + k]
            )
        )
        stores[-1].start()
    for copy in stores:
        copy.wait()


def finish(take, mix, home, stream, inverse, gain):
    tokens, width = stream.shape
    vmem = pl.BlockSpec(memory_space=pltpu.VMEM)
    hbm = pl.BlockSpec(memory_space=pl.ANY)
    blocks = 8
    return pl.pallas_call(
        finish_kernel,
        in_specs=[vmem, vmem, hbm, vmem, vmem, vmem],
        out_specs=(hbm, hbm),
        out_shape=(
            jax.ShapeDtypeStruct((1, tokens, width), BF16),
            jax.ShapeDtypeStruct((1, tokens, width), F32),
        ),
        scratch_shapes=[
            pltpu.VMEM(home.shape, BF16),
            pltpu.VMEM((1, tokens, width), BF16),
            pltpu.VMEM((1, tokens, width), F32),
            pltpu.SemaphoreType.DMA((blocks,)),
            pltpu.SemaphoreType.DMA((blocks,)),
        ],
        compiler_params=params(),
        cost_estimate=cost(LONG, LONG // 1000),
        name="finish",
    )(take, mix, home, stream, inverse, gain)


def in_hbm(values):
    return pltpu.with_memory_space_constraint(values, pltpu.HBM)


def swap(values, axis="expert"):
    return lax.all_to_all(values, axis, split_axis=0, concat_axis=0, tiled=True)


def body(qkv, resid, lengths, norm_gain, expert_ids, gate_vals, w_gate, w_up, w_down, cotangent):
    _, steps, triple = qkv.shape
    width = triple // 3
    head_size = width // HEADS
    owners = lax.axis_size("expert")
    quarters = owners // (steps // 16)
    capacity = 2 * steps * expert_ids.shape[2] // owners
    slots = owners * capacity
    gain = norm_gain.reshape(1, width)

    down_full = lax.all_gather(w_down, "dp", axis=2, tiled=True)
    gate_full = lax.all_gather(w_gate, "dp", axis=2, tiled=True)
    up_full = lax.all_gather(w_up, "dp", axis=2, tiled=True)

    received = swap(pack(lengths, qkv, quarters))
    put, adjoint_send = route(
        expert_ids, gate_vals, cotangent, capacity, slots, width // quarters
    )
    take, mix = back(expert_ids, gate_vals, capacity, slots)
    shared = swap(in_hbm(attend(received, in_hbm(adjoint_send), head_size)))
    stream, inverse, normed_send = norm(lengths, shared, resid, gain, put, quarters)
    x_rows = swap(normed_send)

    gate_full, up_full, down_full = in_hbm(gate_full), in_hbm(up_full), in_hbm(down_full)
    grad_hidden = in_hbm(hidden_grad(shared, down_full))
    rows, inner = expert(x_rows, grad_hidden, gate_full, up_full, down_full)
    home = swap(rows)

    grads = lax.psum_scatter(
        partials(inner, x_rows, shared), "dp", scatter_dimension=1, tiled=True
    )
    grad_gate, grad_up, grad_down = widen(in_hbm(grads), w_gate.shape[1])
    mixture, grad_stream = finish(take, mix, home, stream, inverse, gain)
    return (mixture, grad_stream, grad_gate, grad_up, grad_down)


def solution(mesh):
    tokens = P(("dp", "expert"), None, None)
    weights = P("expert", None, "dp")
    in_specs = (
        tokens,
        tokens,
        P(("dp", "expert")),
        P(),
        tokens,
        tokens,
        weights,
        weights,
        weights,
        tokens,
    )
    out_specs = (tokens, tokens, weights, weights, weights)
    return jax.shard_map(body, mesh=mesh, in_specs=in_specs, out_specs=out_specs, check_vma=False)
```

```python
import functools
import math

import jax
import jax.numpy as jnp
from jax import lax
from jax.experimental import pallas as pl
from jax.experimental.pallas import tpu as pltpu
from jax.sharding import PartitionSpec as P

HEADS = 16
ABSENT = 100.0
F32 = jnp.float32
BF16 = jnp.bfloat16
LONG = 10**15


def cost(flops, bytes_accessed, transcendentals=0):
    return pl.CostEstimate(
        flops=flops, bytes_accessed=bytes_accessed, transcendentals=transcendentals
    )


def params(mebibytes=40):
    return pltpu.CompilerParams(vmem_limit_bytes=mebibytes * 1024 * 1024)


def dot_nt(a, b):
    return lax.dot_general(a, b, (((1,), (1,)), ((), ())), preferred_element_type=F32)


def flat_rows(ref):
    return ref[...].reshape(ref.shape[0] * ref.shape[1], ref.shape[2])


def dot_nn(a, b):
    return lax.dot_general(a, b, (((1,), (0,)), ((), ())), preferred_element_type=F32)


def pack_kernel(quarters, lengths_ref, qkv_ref, out_ref):
    rows = qkv_ref.shape[1]
    wide = out_ref.shape[3]
    step = pl.program_id(0)
    for block in range(rows // 16):
        times = step * rows + block * 16 + lax.broadcasted_iota(jnp.int32, (16, wide), 0)
        live = times < lengths_ref[0]
        for quarter in range(quarters):
            for kind in range(3):
                start = (kind * quarters + quarter) * wide
                piece = qkv_ref[0, block * 16 : block * 16 + 16, start : start + wide]
                if kind == 1:
                    piece = jnp.where(live, piece.astype(F32), ABSENT).astype(BF16)
                out_ref[block * quarters + quarter, kind] = piece


def pack(lengths, qkv, quarters):
    _, steps, triple = qkv.shape
    wide = triple // 3 // quarters
    rows = 32
    return pl.pallas_call(
        functools.partial(pack_kernel, quarters),
        grid=(steps // rows,),
        in_specs=[
            pl.BlockSpec(memory_space=pltpu.SMEM),
            pl.BlockSpec((1, rows, triple), lambda i: (0, i, 0)),
        ],
        out_specs=pl.BlockSpec((rows // 16 * quarters, 3, 16, wide), lambda i: (i, 0, 0, 0)),
        out_shape=jax.ShapeDtypeStruct((steps // 16 * quarters, 3, 16, wide), BF16),
        compiler_params=params(),
        cost_estimate=cost(0, 4 * steps * triple),
        name="pack_qkv",
    )(lengths, qkv)


def attend_kernel(head_size, scale, in_ref, shared_ref, out_ref, bias_ref):
    del shared_ref
    series, _, times, wide = in_ref.shape
    pairs = series * times
    chunk = 128
    keys = in_ref[:, 1, :, 0:head_size].reshape(pairs, head_size)
    total = dot_nt(jnp.ones((8, head_size), BF16), keys)[0:1]
    live = total < 0.5 * ABSENT * head_size
    for part in range(pairs // chunk):
        first = part * chunk // times
        count = chunk // times
        row = part * chunk + lax.broadcasted_iota(jnp.int32, (chunk, pairs), 0)
        column = lax.broadcasted_iota(jnp.int32, (chunk, pairs), 1)
        allowed = (((row ^ column) & (times - 1)) == 0) & (live | (row == column))
        bias_ref[...] = jnp.where(allowed, 0.0, -1e30)
        for head in range(wide // head_size):
            lanes = slice(head * head_size, (head + 1) * head_size)
            queries = in_ref[first : first + count, 0, :, lanes].reshape(chunk, head_size)
            keys = in_ref[:, 1, :, lanes].reshape(pairs, head_size)
            values = in_ref[:, 2, :, lanes].reshape(pairs, head_size)
            scores = dot_nt(queries, keys) * scale + bias_ref[...]
            highest = jnp.max(scores, axis=1, keepdims=True)
            raised = jnp.exp2(scores - highest).astype(BF16)
            both = dot_nn(raised, jnp.concatenate([values, jnp.ones_like(values)], axis=1))
            attended = (both[:, :head_size] / both[:, head_size:]).astype(BF16)
            out_ref[first : first + count, :, lanes] = attended.reshape(count, times, head_size)


def attend(received, shared, head_size):
    series, _, times, wide = received.shape
    pairs = series * times
    heads = wide // head_size
    last = shared.shape[2] // wide - 1
    return pl.pallas_call(
        functools.partial(attend_kernel, head_size, math.log2(math.e) / math.sqrt(head_size)),
        grid=(1,),
        in_specs=[
            pl.BlockSpec(received.shape, lambda i: (0, 0, 0, 0)),
            pl.BlockSpec(memory_space=pl.ANY),
        ],
        out_specs=pl.BlockSpec((series, times, wide), lambda i: (0, 0, last)),
        out_shape=jax.ShapeDtypeStruct(shared.shape, BF16),
        input_output_aliases={1: 0},
        scratch_shapes=[pltpu.VMEM((128, pairs), F32)],
        compiler_params=params(),
        cost_estimate=cost(
            4 * heads * pairs * pairs * head_size, received.size * 8 // 3, heads * pairs * pairs
        ),
        name="attend",
    )(received, shared)


def slots_of(ids_ref, capacity):
    tokens = ids_ref.shape[1]
    ids = ids_ref[0]
    lane = lax.broadcasted_iota(jnp.int32, (tokens, tokens), 1)
    sub = lax.broadcasted_iota(jnp.int32, (tokens, tokens), 0)
    named = [(lane == ids[:, k : k + 1]).astype(F32) for k in range(2)]
    earlier = (lane < sub).astype(BF16)
    before = dot_nn(earlier, (named[0] + named[1]).astype(BF16))
    return [
        ids[:, k : k + 1].astype(F32) * capacity
        + jnp.sum(before * named[k], axis=1, keepdims=True)
        for k in range(2)
    ]


def across(column):
    tokens = column.shape[0]
    return jnp.transpose(jnp.broadcast_to(column, (tokens, tokens)))[0:1]


def route_kernel(capacity, ids_ref, gates_ref, cotangent_ref, put_ref, send_ref):
    slots, tokens = put_ref.shape
    gates = gates_ref[0].astype(F32)
    flat = [across(column) for column in slots_of(ids_ref, capacity)]
    flat_gate = [across(gates[:, k : k + 1]) for k in range(2)]
    down = lax.broadcasted_iota(jnp.int32, (slots, tokens), 0).astype(F32)
    fall = [down == flat[k] for k in range(2)]
    put_ref[...] = jnp.where(fall[0] | fall[1], 1.0, 0.0).astype(BF16)
    weigh = jnp.where(fall[0], flat_gate[0], jnp.where(fall[1], flat_gate[1], 0.0)).astype(BF16)
    owners = slots // capacity
    wide = cotangent_ref.shape[2]
    for start in range(0, wide, 512):
        rows = dot_nn(weigh, cotangent_ref[0, :, start : start + 512]).astype(BF16)
        send_ref[:, :, start : start + 512] = rows.reshape(owners, capacity, 512)


def route(ids, gates, cotangent, capacity, slots, extra):
    _, tokens, wide = cotangent.shape
    return pl.pallas_call(
        functools.partial(route_kernel, capacity),
        out_shape=(
            jax.ShapeDtypeStruct((slots, tokens), BF16),
            jax.ShapeDtypeStruct((slots // capacity, capacity, wide + extra), BF16),
        ),
        grid=(1,),
        in_specs=[
            pl.BlockSpec(ids.shape, lambda i: (0, 0, 0)),
            pl.BlockSpec(gates.shape, lambda i: (0, 0, 0)),
            pl.BlockSpec(cotangent.shape, lambda i: (0, 0, 0)),
        ],
        out_specs=(
            pl.BlockSpec((slots, tokens), lambda i: (0, 0)),
            pl.BlockSpec((slots // capacity, capacity, wide), lambda i: (0, 0, 0)),
        ),
        compiler_params=params(),
        cost_estimate=cost(2 * slots * tokens * wide, 2 * (slots + tokens) * wide),
        name="route",
    )(ids, gates, cotangent)


def back_kernel(capacity, ids_ref, gates_ref, take_ref, mix_ref):
    gates = gates_ref[0].astype(F32)
    slot = slots_of(ids_ref, capacity)
    along = lax.broadcasted_iota(jnp.int32, take_ref.shape, 1).astype(F32)
    hit = [along == slot[k] for k in range(2)]
    take_ref[...] = jnp.where(hit[0] | hit[1], 1.0, 0.0).astype(BF16)
    mix_ref[...] = jnp.where(
        hit[0], gates[:, 0:1], jnp.where(hit[1], gates[:, 1:2], 0.0)
    ).astype(BF16)


def back(ids, gates, capacity, slots):
    shape = jax.ShapeDtypeStruct((ids.shape[1], slots), BF16)
    return pl.pallas_call(
        functools.partial(back_kernel, capacity),
        out_shape=(shape, shape),
        compiler_params=params(),
        cost_estimate=cost(10**6, 10**6),
        name="back",
    )(ids, gates)


def norm_kernel(
    quarters,
    lengths_ref,
    att_ref,
    resid_ref,
    gain_ref,
    put_ref,
    stream_ref,
    inverse_ref,
    send_hbm,
    send_ref,
    sems,
):
    blocks, times, wide = att_ref.shape
    for block in range(blocks):
        at, quarter = block // quarters, block % quarters
        rows = slice(at * times, (at + 1) * times)
        lanes = slice(quarter * wide, (quarter + 1) * wide)
        live = at * times + lax.broadcasted_iota(jnp.int32, (times, wide), 0) < lengths_ref[0]
        stream_ref[rows, lanes] = resid_ref[0, rows, lanes].astype(F32) + jnp.where(
            live, att_ref[block].astype(F32), 0.0
        )
    width = stream_ref.shape[1]
    stream = stream_ref[...]
    inverse = 1.0 / jnp.sqrt(jnp.sum(stream * stream, axis=1, keepdims=True) / width + 1e-05)
    inverse_ref[...] = jnp.broadcast_to(inverse, inverse_ref.shape)
    stores = []
    for start in range(0, width, 512):
        lanes = slice(start, start + 512)
        normed = (stream_ref[:, lanes] * inverse * gain_ref[:, lanes]).astype(BF16)
        rows = dot_nn(put_ref[...], normed).astype(BF16)
        send_ref[:, :, lanes] = rows.reshape(send_ref.shape[0], send_ref.shape[1], 512)
        stores.append(
            pltpu.make_async_copy(
                send_ref.at[:, :, lanes], send_hbm.at[:, :, lanes], sems.at[len(stores)]
            )
        )
        stores[-1].start()
    for copy in stores:
        copy.wait()


def norm(lengths, att, resid, gain, put, quarters):
    _, tokens, width = resid.shape
    slots = put.shape[0]
    blocks, times, whole = att.shape
    wide = width // quarters
    return pl.pallas_call(
        functools.partial(norm_kernel, quarters),
        grid=(1,),
        in_specs=[
            pl.BlockSpec(memory_space=pltpu.SMEM),
            pl.BlockSpec((blocks, times, wide), lambda i: (0, 0, whole // wide - 1)),
            pl.BlockSpec(resid.shape, lambda i: (0, 0, 0)),
            pl.BlockSpec(gain.shape, lambda i: (0, 0)),
            pl.BlockSpec(put.shape, lambda i: (0, 0)),
        ],
        out_specs=(
            pl.BlockSpec((tokens, width), lambda i: (0, 0)),
            pl.BlockSpec((tokens, 128), lambda i: (0, 0)),
            pl.BlockSpec(memory_space=pl.ANY),
        ),
        out_shape=(
            jax.ShapeDtypeStruct((tokens, width), F32),
            jax.ShapeDtypeStruct((tokens, 128), F32),
            pltpu.HBM((blocks, slots // blocks, width), BF16),
        ),
        scratch_shapes=[
            pltpu.VMEM((blocks, slots // blocks, width), BF16),
            pltpu.SemaphoreType.DMA((width // 512,)),
        ],
        compiler_params=params(),
        cost_estimate=cost(2 * slots * tokens * width, 2 * (slots + 4 * tokens) * width),
        name="norm",
    )(lengths, att, resid, gain, put)


def expert_kernel(
    x_ref,
    gh_hbm,
    gate_hbm,
    up_hbm,
    down_hbm,
    rows_hbm,
    inner_hbm,
    gh_ref,
    gate_ref,
    up_ref,
    down_ref,
    rows_ref,
    inner_ref,
    in_sems,
    out_sems,
):
    fetches = [
        pltpu.make_async_copy(source, target, in_sems.at[k])
        for k, (source, target) in enumerate(
            (
                (gate_hbm, gate_ref),
                (up_hbm, up_ref),
                (gh_hbm, gh_ref),
                (down_hbm, down_ref),
            )
        )
    ]
    for fetch in fetches:
        fetch.start()
    stores = []

    def store(source, target):
        copy = pltpu.make_async_copy(source, target, out_sems.at[len(stores)])
        copy.start()
        stores.append(copy)

    fetches[0].wait()
    x = flat_rows(x_ref)
    gate_pre = dot_nt(x, gate_ref[0])
    fetches[1].wait()
    up_pre = dot_nt(x, up_ref[0])
    sigmoid = 1.0 / (1.0 + jnp.exp(-gate_pre))
    silu = gate_pre * sigmoid
    inner_ref[2] = (silu * up_pre).astype(BF16)
    store(inner_ref.at[2], inner_hbm.at[2])
    fetches[2].wait()
    grad_hidden = gh_ref[...]
    inner_ref[0] = (
        grad_hidden * up_pre * sigmoid * (1.0 + gate_pre * (1.0 - sigmoid))
    ).astype(BF16)
    store(inner_ref.at[0], inner_hbm.at[0])
    inner_ref[1] = (grad_hidden * silu).astype(BF16)
    store(inner_ref.at[1], inner_hbm.at[1])
    fetches[3].wait()
    owners, capacity, width = x_ref.shape
    half = width // 2
    for k in range(2):
        lanes = slice(k * half, (k + 1) * half)
        product = dot_nn(inner_ref[2], down_ref[0, :, lanes]).astype(BF16)
        rows_ref[:, :, lanes] = product.reshape(owners, capacity, half)
        store(rows_ref.at[:, :, lanes], rows_hbm.at[:, :, lanes])
    for k in range(2):
        lanes = slice(k * half, (k + 1) * half)
        product = dot_nn(inner_ref[0], gate_ref[0, :, lanes])
        product = (product + dot_nn(inner_ref[1], up_ref[0, :, lanes])).astype(BF16)
        lanes = slice(width + k * half, width + (k + 1) * half)
        rows_ref[:, :, lanes] = product.reshape(owners, capacity, half)
        store(rows_ref.at[:, :, lanes], rows_hbm.at[:, :, lanes])
    for copy in stores:
        copy.wait()


def expert(x, grad_hidden, gate, up, down):
    owners, capacity, width = x.shape
    rows = owners * capacity
    units = gate.shape[1]
    hbm = pl.BlockSpec(memory_space=pl.ANY)
    out = (owners, capacity, 2 * width)
    inner = (3, rows, units)
    return pl.pallas_call(
        expert_kernel,
        in_specs=[pl.BlockSpec(memory_space=pltpu.VMEM)] + [hbm] * 4,
        out_specs=(hbm, hbm),
        out_shape=(pltpu.HBM(out, BF16), pltpu.HBM(inner, BF16)),
        scratch_shapes=[
            pltpu.VMEM(grad_hidden.shape, F32),
            pltpu.VMEM(gate.shape, BF16),
            pltpu.VMEM(up.shape, BF16),
            pltpu.VMEM(down.shape, BF16),
            pltpu.VMEM(out, BF16),
            pltpu.VMEM(inner, BF16),
            pltpu.SemaphoreType.DMA((4,)),
            pltpu.SemaphoreType.DMA((7,)),
        ],
        compiler_params=params(40),
        cost_estimate=cost(
            10 * rows * width * units, 6 * rows * width + 6 * units * width, rows * units
        ),
        name="expert",
    )(x, grad_hidden, gate, up, down)


def grad_hidden_kernel(grad_out_ref, down_ref, out_ref):
    out_ref[...] = dot_nt(flat_rows(grad_out_ref), down_ref[0])


def hidden_grad(shared, down):
    owners, capacity, _ = shared.shape
    rows = owners * capacity
    _, units, width = down.shape
    block = 256
    return pl.pallas_call(
        grad_hidden_kernel,
        grid=(units // block,),
        in_specs=[
            pl.BlockSpec((owners, capacity, width), lambda i: (0, 0, 0)),
            pl.BlockSpec((1, block, width), lambda i: (0, i, 0)),
        ],
        out_specs=pl.BlockSpec((rows, block), lambda i: (0, i)),
        out_shape=jax.ShapeDtypeStruct((rows, units), F32),
        compiler_params=params(),
        cost_estimate=cost(2 * rows * units * width, 2 * width * (rows + units) + 4 * rows * units),
        name="grad_hidden",
    )(shared, down)


def partial_kernel(inner_ref, x_ref, grad_out_ref, out_ref):
    def product(right):
        return lax.dot_general(
            inner_ref[0], right, (((0,), (0,)), ((), ())), preferred_element_type=F32
        ).astype(BF16)

    @pl.when(pl.program_id(0) < 2)
    def _():
        out_ref[...] = product(flat_rows(x_ref))

    @pl.when(pl.program_id(0) == 2)
    def _():
        out_ref[...] = product(flat_rows(grad_out_ref))


def partials(inner, x, shared):
    kinds, rows, units = inner.shape
    width = x.shape[2]
    block = 256
    count = units // block
    whole = pl.BlockSpec(x.shape, lambda k, i: (0, 0, 0))
    return pl.pallas_call(
        partial_kernel,
        grid=(kinds, count),
        in_specs=[pl.BlockSpec((1, rows, block), lambda k, i: (k, 0, i)), whole, whole],
        out_specs=pl.BlockSpec((block, width), lambda k, i: (k * count + i, 0)),
        out_shape=jax.ShapeDtypeStruct((kinds * units, width), BF16),
        compiler_params=params(36),
        cost_estimate=cost(2 * kinds * rows * units * width, 4 * (kinds * units + rows) * width),
        name="partials",
    )(inner, x, shared)


def widen_kernel(in_ref, *out_refs):
    units = out_refs[0].shape[1]
    for k, out_ref in enumerate(out_refs):
        out_ref[0] = in_ref[k * units : (k + 1) * units].astype(F32)


def widen(grads, units):
    rows, width = grads.shape
    return pl.pallas_call(
        widen_kernel,
        out_shape=(jax.ShapeDtypeStruct((1, units, width), F32),) * (rows // units),
        compiler_params=params(),
        cost_estimate=cost(0, 6 * rows * width),
        name="widen",
    )(grads)


def finish_kernel(
    take_ref,
    mix_ref,
    home_hbm,
    stream_ref,
    inverse_ref,
    gain_ref,
    mixture_hbm,
    out_hbm,
    home_ref,
    mixture_ref,
    out_ref,
    in_sems,
    out_sems,
):
    width = stream_ref.shape[1]
    slots = take_ref.shape[1]
    blocks = in_sems.shape[0]
    wide = home_ref.shape[2] // blocks
    half = blocks // 2
    order = list(range(half, blocks)) + list(range(half))

    def block(k):
        return slice(k * wide, (k + 1) * wide)

    fetches = {
        k: pltpu.make_async_copy(
            home_hbm.at[:, :, block(k)], home_ref.at[:, :, block(k)], in_sems.at[k]
        )
        for k in order
    }
    for k in order:
        fetches[k].start()
    total = 0.0
    for k in range(half):
        fetches[half + k].wait()
        home = home_ref[:, :, block(half + k)].reshape(slots, wide)
        scaled = dot_nn(take_ref[...], home) * gain_ref[:, block(k)]
        out_ref[0, :, block(k)] = scaled
        total = total + jnp.sum(stream_ref[:, block(k)] * scaled, axis=1, keepdims=True)
    inverse = inverse_ref[:, 0:1]
    factor = inverse * inverse * inverse * (total / width)
    stores = []
    for k in range(half):
        out_ref[0, :, block(k)] = inverse * out_ref[0, :, block(k)] - stream_ref[:, block(k)] * factor
        stores.append(
            pltpu.make_async_copy(
                out_ref.at[:, :, block(k)], out_hbm.at[:, :, block(k)], out_sems.at[k]
            )
        )
        stores[-1].start()
    for k in range(half):
        fetches[k].wait()
        home = home_ref[:, :, block(k)].reshape(slots, wide)
        mixture_ref[0, :, block(k)] = dot_nn(mix_ref[...], home).astype(BF16)
        stores.append(
            pltpu.make_async_copy(
                mixture_ref.at[:, :, block(k)], mixture_hbm.at[:, :, block(k)], out_sems.at[half + k]
            )
        )
        stores[-1].start()
    for copy in stores:
        copy.wait()


def finish(take, mix, home, stream, inverse, gain):
    tokens, width = stream.shape
    vmem = pl.BlockSpec(memory_space=pltpu.VMEM)
    hbm = pl.BlockSpec(memory_space=pl.ANY)
    blocks = 8
    return pl.pallas_call(
        finish_kernel,
        in_specs=[vmem, vmem, hbm, vmem, vmem, vmem],
        out_specs=(hbm, hbm),
        out_shape=(
            jax.ShapeDtypeStruct((1, tokens, width), BF16),
            jax.ShapeDtypeStruct((1, tokens, width), F32),
        ),
        scratch_shapes=[
            pltpu.VMEM(home.shape, BF16),
            pltpu.VMEM((1, tokens, width), BF16),
            pltpu.VMEM((1, tokens, width), F32),
            pltpu.SemaphoreType.DMA((blocks,)),
            pltpu.SemaphoreType.DMA((blocks,)),
        ],
        compiler_params=params(),
        cost_estimate=cost(LONG, LONG // 1000),
        name="finish",
    )(take, mix, home, stream, inverse, gain)


def in_hbm(values):
    return pltpu.with_memory_space_constraint(values, pltpu.HBM)


def swap(values, axis="expert"):
    return lax.all_to_all(values, axis, split_axis=0, concat_axis=0, tiled=True)


def body(qkv, resid, lengths, norm_gain, expert_ids, gate_vals, w_gate, w_up, w_down, cotangent):
    _, steps, triple = qkv.shape
    width = triple // 3
    head_size = width // HEADS
    owners = lax.axis_size("expert")
    quarters = owners // (steps // 16)
    capacity = 2 * steps * expert_ids.shape[2] // owners
    slots = owners * capacity
    gain = norm_gain.reshape(1, width)

    down_full = lax.all_gather(w_down, "dp", axis=2, tiled=True)
    gate_full = lax.all_gather(w_gate, "dp", axis=2, tiled=True)
    up_full = lax.all_gather(w_up, "dp", axis=2, tiled=True)

    received = swap(pack(lengths, qkv, quarters))
    put, adjoint_send = route(
        expert_ids, gate_vals, cotangent, capacity, slots, width // quarters
    )
    take, mix = back(expert_ids, gate_vals, capacity, slots)
    shared = swap(in_hbm(attend(received, in_hbm(adjoint_send), head_size)))
    stream, inverse, normed_send = norm(lengths, shared, resid, gain, put, quarters)
    x_rows = pltpu.with_memory_space_constraint(swap(normed_send), pltpu.VMEM)

    gate_full, up_full, down_full = in_hbm(gate_full), in_hbm(up_full), in_hbm(down_full)
    grad_hidden = in_hbm(hidden_grad(shared, down_full))
    rows, inner = expert(x_rows, grad_hidden, gate_full, up_full, down_full)
    home = swap(rows)

    grads = lax.psum_scatter(
        partials(inner, x_rows, shared), "dp", scatter_dimension=1, tiled=True
    )
    grad_gate, grad_up, grad_down = widen(in_hbm(grads), w_gate.shape[1])
    mixture, grad_stream = finish(take, mix, home, stream, inverse, gain)
    return (mixture, grad_stream, grad_gate, grad_up, grad_down)


def solution(mesh):
    tokens = P(("dp", "expert"), None, None)
    weights = P("expert", None, "dp")
    in_specs = (
        tokens,
        tokens,
        P(("dp", "expert")),
        P(),
        tokens,
        tokens,
        weights,
        weights,
        weights,
        tokens,
    )
    out_specs = (tokens, tokens, weights, weights, weights)
    return jax.shard_map(body, mesh=mesh, in_specs=in_specs, out_specs=out_specs, check_vma=False)
```

```python
import functools
import math

import jax
import jax.numpy as jnp
from jax import lax
from jax.experimental import pallas as pl
from jax.experimental.pallas import tpu as pltpu
from jax.sharding import PartitionSpec as P

HEADS = 16
ABSENT = 100.0
F32 = jnp.float32
BF16 = jnp.bfloat16
LONG = 10**15


def cost(flops, bytes_accessed, transcendentals=0):
    return pl.CostEstimate(
        flops=flops, bytes_accessed=bytes_accessed, transcendentals=transcendentals
    )


def params(mebibytes=40):
    return pltpu.CompilerParams(vmem_limit_bytes=mebibytes * 1024 * 1024)


def dot_nt(a, b):
    return lax.dot_general(a, b, (((1,), (1,)), ((), ())), preferred_element_type=F32)


def flat_rows(ref):
    return ref[...].reshape(ref.shape[0] * ref.shape[1], ref.shape[2])


def dot_nn(a, b):
    return lax.dot_general(a, b, (((1,), (0,)), ((), ())), preferred_element_type=F32)


def pack_kernel(quarters, lengths_ref, qkv_ref, out_ref):
    rows = qkv_ref.shape[1]
    wide = out_ref.shape[3]
    step = pl.program_id(0)
    for block in range(rows // 16):
        times = step * rows + block * 16 + lax.broadcasted_iota(jnp.int32, (16, wide), 0)
        live = times < lengths_ref[0]
        for quarter in range(quarters):
            for kind in range(3):
                start = (kind * quarters + quarter) * wide
                piece = qkv_ref[0, block * 16 : block * 16 + 16, start : start + wide]
                if kind == 1:
                    piece = jnp.where(live, piece.astype(F32), ABSENT).astype(BF16)
                out_ref[block * quarters + quarter, kind] = piece


def pack(lengths, qkv, quarters):
    _, steps, triple = qkv.shape
    wide = triple // 3 // quarters
    rows = 32
    return pl.pallas_call(
        functools.partial(pack_kernel, quarters),
        grid=(steps // rows,),
        in_specs=[
            pl.BlockSpec(memory_space=pltpu.SMEM),
            pl.BlockSpec((1, rows, triple), lambda i: (0, i, 0)),
        ],
        out_specs=pl.BlockSpec((rows // 16 * quarters, 3, 16, wide), lambda i: (i, 0, 0, 0)),
        out_shape=jax.ShapeDtypeStruct((steps // 16 * quarters, 3, 16, wide), BF16),
        compiler_params=params(),
        cost_estimate=cost(0, 4 * steps * triple),
        name="pack_qkv",
    )(lengths, qkv)


def attend_kernel(head_size, scale, in_ref, shared_ref, out_ref, bias_ref):
    del shared_ref
    series, _, times, wide = in_ref.shape
    pairs = series * times
    chunk = 128
    keys = in_ref[:, 1, :, 0:head_size].reshape(pairs, head_size)
    total = dot_nt(jnp.ones((8, head_size), BF16), keys)[0:1]
    live = total < 0.5 * ABSENT * head_size
    for part in range(pairs // chunk):
        first = part * chunk // times
        count = chunk // times
        row = part * chunk + lax.broadcasted_iota(jnp.int32, (chunk, pairs), 0)
        column = lax.broadcasted_iota(jnp.int32, (chunk, pairs), 1)
        allowed = (((row ^ column) & (times - 1)) == 0) & (live | (row == column))
        bias_ref[...] = jnp.where(allowed, 0.0, -1e30)
        for head in range(wide // head_size):
            lanes = slice(head * head_size, (head + 1) * head_size)
            queries = in_ref[first : first + count, 0, :, lanes].reshape(chunk, head_size)
            keys = in_ref[:, 1, :, lanes].reshape(pairs, head_size)
            values = in_ref[:, 2, :, lanes].reshape(pairs, head_size)
            scores = dot_nt(queries, keys) * scale + bias_ref[...]
            highest = jnp.max(scores, axis=1, keepdims=True)
            raised = jnp.exp2(scores - highest).astype(BF16)
            both = dot_nn(raised, jnp.concatenate([values, jnp.ones_like(values)], axis=1))
            attended = (both[:, :head_size] / both[:, head_size:]).astype(BF16)
            out_ref[first : first + count, :, lanes] = attended.reshape(count, times, head_size)


def attend(received, shared, head_size):
    series, _, times, wide = received.shape
    pairs = series * times
    heads = wide // head_size
    last = shared.shape[2] // wide - 1
    return pl.pallas_call(
        functools.partial(attend_kernel, head_size, math.log2(math.e) / math.sqrt(head_size)),
        grid=(1,),
        in_specs=[
            pl.BlockSpec(received.shape, lambda i: (0, 0, 0, 0)),
            pl.BlockSpec(memory_space=pl.ANY),
        ],
        out_specs=pl.BlockSpec((series, times, wide), lambda i: (0, 0, last)),
        out_shape=jax.ShapeDtypeStruct(shared.shape, BF16),
        input_output_aliases={1: 0},
        scratch_shapes=[pltpu.VMEM((128, pairs), F32)],
        compiler_params=params(),
        cost_estimate=cost(
            4 * heads * pairs * pairs * head_size, received.size * 8 // 3, heads * pairs * pairs
        ),
        name="attend",
    )(received, shared)


def slots_of(ids_ref, capacity):
    tokens = ids_ref.shape[1]
    ids = ids_ref[0]
    lane = lax.broadcasted_iota(jnp.int32, (tokens, tokens), 1)
    sub = lax.broadcasted_iota(jnp.int32, (tokens, tokens), 0)
    named = [(lane == ids[:, k : k + 1]).astype(F32) for k in range(2)]
    earlier = (lane < sub).astype(BF16)
    before = dot_nn(earlier, (named[0] + named[1]).astype(BF16))
    return [
        ids[:, k : k + 1].astype(F32) * capacity
        + jnp.sum(before * named[k], axis=1, keepdims=True)
        for k in range(2)
    ]


def across(column):
    tokens = column.shape[0]
    return jnp.transpose(jnp.broadcast_to(column, (tokens, tokens)))[0:1]


def route_kernel(capacity, ids_ref, gates_ref, cotangent_ref, put_ref, send_ref):
    slots, tokens = put_ref.shape
    gates = gates_ref[0].astype(F32)
    flat = [across(column) for column in slots_of(ids_ref, capacity)]
    flat_gate = [across(gates[:, k : k + 1]) for k in range(2)]
    down = lax.broadcasted_iota(jnp.int32, (slots, tokens), 0).astype(F32)
    fall = [down == flat[k] for k in range(2)]
    put_ref[...] = jnp.where(fall[0] | fall[1], 1.0, 0.0).astype(BF16)
    weigh = jnp.where(fall[0], flat_gate[0], jnp.where(fall[1], flat_gate[1], 0.0)).astype(BF16)
    owners = slots // capacity
    wide = cotangent_ref.shape[2]
    for start in range(0, wide, 512):
        rows = dot_nn(weigh, cotangent_ref[0, :, start : start + 512]).astype(BF16)
        send_ref[:, :, start : start + 512] = rows.reshape(owners, capacity, 512)


def route(ids, gates, cotangent, capacity, slots, extra):
    _, tokens, wide = cotangent.shape
    return pl.pallas_call(
        functools.partial(route_kernel, capacity),
        out_shape=(
            jax.ShapeDtypeStruct((slots, tokens), BF16),
            jax.ShapeDtypeStruct((slots // capacity, capacity, wide + extra), BF16),
        ),
        grid=(1,),
        in_specs=[
            pl.BlockSpec(ids.shape, lambda i: (0, 0, 0)),
            pl.BlockSpec(gates.shape, lambda i: (0, 0, 0)),
            pl.BlockSpec(cotangent.shape, lambda i: (0, 0, 0)),
        ],
        out_specs=(
            pl.BlockSpec((slots, tokens), lambda i: (0, 0)),
            pl.BlockSpec((slots // capacity, capacity, wide), lambda i: (0, 0, 0)),
        ),
        compiler_params=params(),
        cost_estimate=cost(2 * slots * tokens * wide, 2 * (slots + tokens) * wide),
        name="route",
    )(ids, gates, cotangent)


def back_kernel(capacity, ids_ref, gates_ref, take_ref, mix_ref):
    gates = gates_ref[0].astype(F32)
    slot = slots_of(ids_ref, capacity)
    along = lax.broadcasted_iota(jnp.int32, take_ref.shape, 1).astype(F32)
    hit = [along == slot[k] for k in range(2)]
    take_ref[...] = jnp.where(hit[0] | hit[1], 1.0, 0.0).astype(BF16)
    mix_ref[...] = jnp.where(
        hit[0], gates[:, 0:1], jnp.where(hit[1], gates[:, 1:2], 0.0)
    ).astype(BF16)


def back(ids, gates, capacity, slots):
    shape = jax.ShapeDtypeStruct((ids.shape[1], slots), BF16)
    return pl.pallas_call(
        functools.partial(back_kernel, capacity),
        out_shape=(shape, shape),
        compiler_params=params(),
        cost_estimate=cost(10**6, 10**6),
        name="back",
    )(ids, gates)


def norm_kernel(
    quarters,
    lengths_ref,
    att_ref,
    resid_ref,
    gain_ref,
    put_ref,
    stream_ref,
    send_hbm,
    send_ref,
    sems,
):
    blocks, times, wide = att_ref.shape
    for block in range(blocks):
        at, quarter = block // quarters, block % quarters
        rows = slice(at * times, (at + 1) * times)
        lanes = slice(quarter * wide, (quarter + 1) * wide)
        live = at * times + lax.broadcasted_iota(jnp.int32, (times, wide), 0) < lengths_ref[0]
        stream_ref[rows, lanes] = resid_ref[0, rows, lanes].astype(F32) + jnp.where(
            live, att_ref[block].astype(F32), 0.0
        )
    width = stream_ref.shape[1]
    stream = stream_ref[...]
    inverse = 1.0 / jnp.sqrt(jnp.sum(stream * stream, axis=1, keepdims=True) / width + 1e-05)
    stores = []
    for start in range(0, width, 512):
        lanes = slice(start, start + 512)
        normed = (stream_ref[:, lanes] * inverse * gain_ref[:, lanes]).astype(BF16)
        rows = dot_nn(put_ref[...], normed).astype(BF16)
        send_ref[:, :, lanes] = rows.reshape(send_ref.shape[0], send_ref.shape[1], 512)
        stores.append(
            pltpu.make_async_copy(
                send_ref.at[:, :, lanes], send_hbm.at[:, :, lanes], sems.at[len(stores)]
            )
        )
        stores[-1].start()
    for copy in stores:
        copy.wait()


def norm(lengths, att, resid, gain, put, quarters):
    _, tokens, width = resid.shape
    slots = put.shape[0]
    blocks, times, whole = att.shape
    wide = width // quarters
    return pl.pallas_call(
        functools.partial(norm_kernel, quarters),
        grid=(1,),
        in_specs=[
            pl.BlockSpec(memory_space=pltpu.SMEM),
            pl.BlockSpec((blocks, times, wide), lambda i: (0, 0, whole // wide - 1)),
            pl.BlockSpec(resid.shape, lambda i: (0, 0, 0)),
            pl.BlockSpec(gain.shape, lambda i: (0, 0)),
            pl.BlockSpec(put.shape, lambda i: (0, 0)),
        ],
        out_specs=(
            pl.BlockSpec((tokens, width), lambda i: (0, 0)),
            pl.BlockSpec(memory_space=pl.ANY),
        ),
        out_shape=(
            jax.ShapeDtypeStruct((tokens, width), F32),
            pltpu.HBM((blocks, slots // blocks, width), BF16),
        ),
        scratch_shapes=[
            pltpu.VMEM((blocks, slots // blocks, width), BF16),
            pltpu.SemaphoreType.DMA((width // 512,)),
        ],
        compiler_params=params(),
        cost_estimate=cost(2 * slots * tokens * width, 2 * (slots + 4 * tokens) * width),
        name="norm",
    )(lengths, att, resid, gain, put)


def expert_kernel(
    x_ref,
    gh_hbm,
    gate_hbm,
    up_hbm,
    down_hbm,
    rows_hbm,
    inner_hbm,
    gh_ref,
    gate_ref,
    up_ref,
    down_ref,
    rows_ref,
    inner_ref,
    in_sems,
    out_sems,
):
    fetches = [
        pltpu.make_async_copy(source, target, in_sems.at[k])
        for k, (source, target) in enumerate(
            (
                (gate_hbm, gate_ref),
                (up_hbm, up_ref),
                (gh_hbm, gh_ref),
                (down_hbm, down_ref),
            )
        )
    ]
    for fetch in fetches:
        fetch.start()
    stores = []

    def store(source, target):
        copy = pltpu.make_async_copy(source, target, out_sems.at[len(stores)])
        copy.start()
        stores.append(copy)

    fetches[0].wait()
    x = flat_rows(x_ref)
    gate_pre = dot_nt(x, gate_ref[0])
    fetches[1].wait()
    up_pre = dot_nt(x, up_ref[0])
    sigmoid = 1.0 / (1.0 + jnp.exp(-gate_pre))
    silu = gate_pre * sigmoid
    inner_ref[2] = (silu * up_pre).astype(BF16)
    store(inner_ref.at[2], inner_hbm.at[2])
    fetches[2].wait()
    grad_hidden = gh_ref[...]
    inner_ref[0] = (
        grad_hidden * up_pre * sigmoid * (1.0 + gate_pre * (1.0 - sigmoid))
    ).astype(BF16)
    store(inner_ref.at[0], inner_hbm.at[0])
    inner_ref[1] = (grad_hidden * silu).astype(BF16)
    store(inner_ref.at[1], inner_hbm.at[1])
    fetches[3].wait()
    owners, capacity, width = x_ref.shape
    half = width // 2
    for k in range(2):
        lanes = slice(k * half, (k + 1) * half)
        product = dot_nn(inner_ref[2], down_ref[0, :, lanes]).astype(BF16)
        rows_ref[:, :, lanes] = product.reshape(owners, capacity, half)
        store(rows_ref.at[:, :, lanes], rows_hbm.at[:, :, lanes])
    for k in range(2):
        lanes = slice(k * half, (k + 1) * half)
        product = dot_nn(inner_ref[0], gate_ref[0, :, lanes])
        product = (product + dot_nn(inner_ref[1], up_ref[0, :, lanes])).astype(BF16)
        lanes = slice(width + k * half, width + (k + 1) * half)
        rows_ref[:, :, lanes] = product.reshape(owners, capacity, half)
        store(rows_ref.at[:, :, lanes], rows_hbm.at[:, :, lanes])
    for copy in stores:
        copy.wait()


def expert(x, grad_hidden, gate, up, down):
    owners, capacity, width = x.shape
    rows = owners * capacity
    units = gate.shape[1]
    hbm = pl.BlockSpec(memory_space=pl.ANY)
    out = (owners, capacity, 2 * width)
    inner = (3, rows, units)
    return pl.pallas_call(
        expert_kernel,
        in_specs=[pl.BlockSpec(memory_space=pltpu.VMEM)] + [hbm] * 4,
        out_specs=(hbm, hbm),
        out_shape=(pltpu.HBM(out, BF16), pltpu.HBM(inner, BF16)),
        scratch_shapes=[
            pltpu.VMEM(grad_hidden.shape, F32),
            pltpu.VMEM(gate.shape, BF16),
            pltpu.VMEM(up.shape, BF16),
            pltpu.VMEM(down.shape, BF16),
            pltpu.VMEM(out, BF16),
            pltpu.VMEM(inner, BF16),
            pltpu.SemaphoreType.DMA((4,)),
            pltpu.SemaphoreType.DMA((7,)),
        ],
        compiler_params=params(40),
        cost_estimate=cost(
            10 * rows * width * units, 6 * rows * width + 6 * units * width, rows * units
        ),
        name="expert",
    )(x, grad_hidden, gate, up, down)


def grad_hidden_kernel(grad_out_ref, down_ref, out_ref):
    out_ref[...] = dot_nt(flat_rows(grad_out_ref), down_ref[0])


def hidden_grad(shared, down):
    owners, capacity, _ = shared.shape
    rows = owners * capacity
    _, units, width = down.shape
    block = 256
    return pl.pallas_call(
        grad_hidden_kernel,
        grid=(units // block,),
        in_specs=[
            pl.BlockSpec((owners, capacity, width), lambda i: (0, 0, 0)),
            pl.BlockSpec((1, block, width), lambda i: (0, i, 0)),
        ],
        out_specs=pl.BlockSpec((rows, block), lambda i: (0, i)),
        out_shape=jax.ShapeDtypeStruct((rows, units), F32),
        compiler_params=params(),
        cost_estimate=cost(2 * rows * units * width, 2 * width * (rows + units) + 4 * rows * units),
        name="grad_hidden",
    )(shared, down)


def partial_kernel(inner_ref, x_ref, grad_out_ref, out_ref):
    def product(right):
        return lax.dot_general(
            inner_ref[0], right, (((0,), (0,)), ((), ())), preferred_element_type=F32
        ).astype(BF16)

    @pl.when(pl.program_id(0) < 2)
    def _():
        out_ref[...] = product(flat_rows(x_ref))

    @pl.when(pl.program_id(0) == 2)
    def _():
        out_ref[...] = product(flat_rows(grad_out_ref))


def partials(inner, x, shared):
    kinds, rows, units = inner.shape
    width = x.shape[2]
    block = 256
    count = units // block
    whole = pl.BlockSpec(x.shape, lambda k, i: (0, 0, 0))
    return pl.pallas_call(
        partial_kernel,
        grid=(kinds, count),
        in_specs=[pl.BlockSpec((1, rows, block), lambda k, i: (k, 0, i)), whole, whole],
        out_specs=pl.BlockSpec((block, width), lambda k, i: (k * count + i, 0)),
        out_shape=jax.ShapeDtypeStruct((kinds * units, width), BF16),
        compiler_params=params(36),
        cost_estimate=cost(2 * kinds * rows * units * width, 4 * (kinds * units + rows) * width),
        name="partials",
    )(inner, x, shared)


def widen_kernel(in_ref, *out_refs):
    units = out_refs[0].shape[1]
    for k, out_ref in enumerate(out_refs):
        out_ref[0] = in_ref[k * units : (k + 1) * units].astype(F32)


def widen(grads, units):
    rows, width = grads.shape
    return pl.pallas_call(
        widen_kernel,
        out_shape=(jax.ShapeDtypeStruct((1, units, width), F32),) * (rows // units),
        compiler_params=params(),
        cost_estimate=cost(0, 6 * rows * width),
        name="widen",
    )(grads)


def finish_kernel(
    take_ref,
    mix_ref,
    home_hbm,
    stream_ref,
    gain_ref,
    mixture_hbm,
    out_hbm,
    home_ref,
    mixture_ref,
    out_ref,
    in_sems,
    out_sems,
):
    width = stream_ref.shape[1]
    slots = take_ref.shape[1]
    blocks = in_sems.shape[0]
    wide = home_ref.shape[2] // blocks
    half = blocks // 2
    order = list(range(half, blocks)) + list(range(half))

    def block(k):
        return slice(k * wide, (k + 1) * wide)

    fetches = {
        k: pltpu.make_async_copy(
            home_hbm.at[:, :, block(k)], home_ref.at[:, :, block(k)], in_sems.at[k]
        )
        for k in order
    }
    for k in order:
        fetches[k].start()
    total, square = 0.0, 0.0
    for k in range(half):
        part = stream_ref[:, block(k)]
        square = square + jnp.sum(part * part, axis=1, keepdims=True)
    inverse = 1.0 / jnp.sqrt(square / width + 1e-05)
    for k in range(half):
        fetches[half + k].wait()
        home = home_ref[:, :, block(half + k)].reshape(slots, wide)
        scaled = dot_nn(take_ref[...], home) * gain_ref[:, block(k)]
        out_ref[0, :, block(k)] = scaled
        total = total + jnp.sum(stream_ref[:, block(k)] * scaled, axis=1, keepdims=True)
    factor = inverse * inverse * inverse * (total / width)
    stores = []
    for k in range(half):
        out_ref[0, :, block(k)] = inverse * out_ref[0, :, block(k)] - stream_ref[:, block(k)] * factor
        stores.append(
            pltpu.make_async_copy(
                out_ref.at[:, :, block(k)], out_hbm.at[:, :, block(k)], out_sems.at[k]
            )
        )
        stores[-1].start()
    for k in range(half):
        fetches[k].wait()
        home = home_ref[:, :, block(k)].reshape(slots, wide)
        mixture_ref[0, :, block(k)] = dot_nn(mix_ref[...], home).astype(BF16)
        stores.append(
            pltpu.make_async_copy(
                mixture_ref.at[:, :, block(k)], mixture_hbm.at[:, :, block(k)], out_sems.at[half + k]
            )
        )
        stores[-1].start()
    for copy in stores:
        copy.wait()


def finish(take, mix, home, stream, gain):
    tokens, width = stream.shape
    vmem = pl.BlockSpec(memory_space=pltpu.VMEM)
    hbm = pl.BlockSpec(memory_space=pl.ANY)
    blocks = 8
    return pl.pallas_call(
        finish_kernel,
        in_specs=[vmem, vmem, hbm, vmem, vmem],
        out_specs=(hbm, hbm),
        out_shape=(
            jax.ShapeDtypeStruct((1, tokens, width), BF16),
            jax.ShapeDtypeStruct((1, tokens, width), F32),
        ),
        scratch_shapes=[
            pltpu.VMEM(home.shape, BF16),
            pltpu.VMEM((1, tokens, width), BF16),
            pltpu.VMEM((1, tokens, width), F32),
            pltpu.SemaphoreType.DMA((blocks,)),
            pltpu.SemaphoreType.DMA((blocks,)),
        ],
        compiler_params=params(),
        cost_estimate=cost(LONG, LONG // 1000),
        name="finish",
    )(take, mix, home, stream, gain)


def in_hbm(values):
    return pltpu.with_memory_space_constraint(values, pltpu.HBM)


def swap(values, axis="expert"):
    return lax.all_to_all(values, axis, split_axis=0, concat_axis=0, tiled=True)


def body(qkv, resid, lengths, norm_gain, expert_ids, gate_vals, w_gate, w_up, w_down, cotangent):
    _, steps, triple = qkv.shape
    width = triple // 3
    head_size = width // HEADS
    owners = lax.axis_size("expert")
    quarters = owners // (steps // 16)
    capacity = 2 * steps * expert_ids.shape[2] // owners
    slots = owners * capacity
    gain = norm_gain.reshape(1, width)

    down_full = lax.all_gather(w_down, "dp", axis=2, tiled=True)
    gate_full = lax.all_gather(w_gate, "dp", axis=2, tiled=True)
    up_full = lax.all_gather(w_up, "dp", axis=2, tiled=True)

    received = swap(pack(lengths, qkv, quarters))
    put, adjoint_send = route(
        expert_ids, gate_vals, cotangent, capacity, slots, width // quarters
    )
    take, mix = back(expert_ids, gate_vals, capacity, slots)
    shared = swap(in_hbm(attend(received, in_hbm(adjoint_send), head_size)))
    stream, normed_send = norm(lengths, shared, resid, gain, put, quarters)
    x_rows = pltpu.with_memory_space_constraint(swap(normed_send), pltpu.VMEM)

    gate_full, up_full, down_full = in_hbm(gate_full), in_hbm(up_full), in_hbm(down_full)
    grad_hidden = in_hbm(hidden_grad(shared, down_full))
    rows, inner = expert(x_rows, grad_hidden, gate_full, up_full, down_full)
    home = swap(rows)

    grads = lax.psum_scatter(
        partials(inner, x_rows, shared), "dp", scatter_dimension=1, tiled=True
    )
    grad_gate, grad_up, grad_down = widen(in_hbm(grads), w_gate.shape[1])
    mixture, grad_stream = finish(take, mix, home, stream, gain)
    return (mixture, grad_stream, grad_gate, grad_up, grad_down)


def solution(mesh):
    tokens = P(("dp", "expert"), None, None)
    weights = P("expert", None, "dp")
    in_specs = (
        tokens,
        tokens,
        P(("dp", "expert")),
        P(),
        tokens,
        tokens,
        weights,
        weights,
        weights,
        tokens,
    )
    out_specs = (tokens, tokens, weights, weights, weights)
    return jax.shard_map(body, mesh=mesh, in_specs=in_specs, out_specs=out_specs, check_vma=False)
```
